32 devices in a mesh: shard: 4 (over y, x), ctx: 2 (over core), tp: 4 (over z).
Axes of the slice: x: 2, y: 2, z: 4, core: 2. Of those that a mesh axis runs over, the one named last changes fastest.
Arguments:
- tokens: bfloat16 [4, 1024, 1536], P('shard', ('ctx', 'tp')), may hold values from -6 to 6
- cotangent: bfloat16 [4, 1024, 1536], P('shard', ('ctx', 'tp')), may hold values from -6 to 6
- lengths: int32 [4], P('shard'), may hold values from 256 to 1024, as said below
- w_qkv: bfloat16 [1536, 3, 1536], P(('shard', 'ctx'), None, 'tp'), may hold values from -0.15625 to 0.15625
- w_forget: bfloat16 [1536, 24], P(('shard', 'ctx'), 'tp'), may hold values from -0.15625 to 0.15625
- forget_bias: float32 [24], replicated, may hold values from 3 to 8
- w_ogate: bfloat16 [1536, 1536], P(('shard', 'ctx'), 'tp'), may hold values from -0.15625 to 0.15625
- w_out: bfloat16 [1536, 1536], P(('shard', 'ctx'), 'tp'), may hold values from -0.625 to 0.625
- w_gu: bfloat16 [1536, 2, 4096], P(('shard', 'ctx'), None, 'tp'), may hold values from -0.15625 to 0.15625
- w_down: bfloat16 [1536, 4096], P(('shard', 'ctx'), 'tp'), may hold values from -0.09375 to 0.09375
- gain_attn: float32 [1536], replicated, may hold values from 0.5 to 1.5
- gain_mlp: float32 [1536], replicated, may hold values from 0.5 to 1.5
- qk_gain: float32 [2, 64], replicated, may hold values from 1 to 2
Outputs:
- output: bfloat16 [4, 1024, 1536], P('shard', ('ctx', 'tp'))
- input_grad: bfloat16 [4, 1024, 1536], P('shard', ('ctx', 'tp'))
- grad_qkv: float32 [1536, 3, 1536], P(('shard', 'ctx'), None, 'tp')
- grad_forget: float32 [1536, 24], P(('shard', 'ctx'), 'tp')
- grad_forget_bias: float32 [24], replicated
- grad_ogate: float32 [1536, 1536], P(('shard', 'ctx'), 'tp')
- grad_out: float32 [1536, 1536], P(('shard', 'ctx'), 'tp')
- grad_gu: float32 [1536, 2, 4096], P(('shard', 'ctx'), None, 'tp')
- grad_down: float32 [1536, 4096], P(('shard', 'ctx'), 'tp')
- grad_gain_attn: float32 [1536], replicated
- grad_gain_mlp: float32 [1536], replicated
- grad_qk_gain: float32 [2, 64], replicated
The draws below stay inside these ranges and needn't reach their ends.
Inputs may be any that keep to these rules, and one draw needn't show every extreme that they name: `lengths`: real tokens of a slot; positions at or past it are padding; both the least and the most value occur in every draw.
All inputs are finite; a program needn't handle non-finite values.
Results may differ from the reference program's by a relative error of at most 0.04.
Values may be sent and summed in bfloat16 or wider, within the bound.
No kernel may reach another device: no remote copies, remote signals or barrier semaphores. Data moves between devices by JAX's collectives and lax.ppermute only.
A program may use at most 128 MiB of HBM per device.

```python
import jax
import jax.numpy as jnp
from jax import lax

D = 1536
HEADS = 24
HEAD = 64
FF = 4096
LEN = 1024
SLOTS = 4


def draw_lengths(key, part):
    first_key, second_key = jax.random.split(key)
    picked = jax.random.randint(first_key, (SLOTS,), LEN // 4, LEN + 1)
    ranking = jax.random.permutation(second_key, SLOTS)
    picked = jnp.where(ranking == 0, LEN, picked)
    picked = jnp.where(ranking == 1, LEN // 4, picked)
    return picked.astype(jnp.int32)


def level_of(own_key, extent, cuts, low, top_value):
    factor_of = 1.0
    for axis_at, parts in cuts:
        heights = jax.random.uniform(jax.random.fold_in(jax.random.fold_in(own_key, 6), axis_at), (parts,), jnp.float32, low / len(cuts), top_value / len(cuts))
        factor_of = factor_of * jnp.repeat(jnp.exp(heights), extent[axis_at] // parts).reshape((-1,) + (1,) * (len(extent) - 1 - axis_at))
    return factor_of


def normal_values(stream_key, dims, spread, bound, cuts=(), held_as=jnp.bfloat16):
    values = jax.random.normal(stream_key, dims, jnp.float32) * spread
    if len(cuts) > 0:
        values = level_of(stream_key, dims, cuts, -0.22, 0.18) * values
    return jnp.clip(values, min=-bound, max=bound).astype(held_as)


def setup_inputs(seed: int = 0) -> dict:
    splits = jax.random.split(jax.random.key(seed), 14)
    tokens = normal_values(splits[0], (SLOTS, LEN, D), 1.0, 6.0, ((0, 4), (1, 8)))
    cotangent = normal_values(splits[1], (SLOTS, LEN, D), 1.0, 6.0, ((0, 4), (1, 8)))
    lengths = draw_lengths(jax.random.fold_in(splits[13], 71), 0)
    w_qkv = normal_values(splits[3], (D, 3, HEADS * HEAD), D ** -0.5, 0.15625, ((0, 8), (2, 4)))
    w_forget = normal_values(splits[4], (D, HEADS), D ** -0.5, 0.15625, ((0, 8), (1, 4)))
    forget_bias = jnp.clip(jax.random.uniform(splits[5], (HEADS,), jnp.float32, 3.0, 8.0), 3.0, 8.0)
    w_ogate = normal_values(splits[6], (D, HEADS * HEAD), D ** -0.5, 0.15625, ((0, 8), (1, 4)))
    w_out = normal_values(splits[7], (D, HEADS * HEAD), (HEADS * HEAD // 16) ** -0.5, 0.625, ((0, 8), (1, 4)))
    w_gu = normal_values(splits[8], (D, 2, FF), D ** -0.5, 0.15625, ((0, 8), (2, 4)))
    w_down = normal_values(splits[9], (D, FF), FF ** -0.5, 0.09375, ((0, 8), (1, 4)))
    gain_attn = jnp.clip(1.0 + 0.1 * jax.random.normal(splits[10], (D,), jnp.float32), 0.5, 1.5)
    gain_mlp = jnp.clip(1.0 + 0.1 * jax.random.normal(splits[11], (D,), jnp.float32), 0.5, 1.5)
    qk_gain = jnp.clip(jax.random.uniform(splits[12], (2, HEAD), jnp.float32, 1.0, 2.0), 1.0, 2.0)
    return dict(tokens=tokens, cotangent=cotangent, lengths=lengths, w_qkv=w_qkv, w_forget=w_forget, forget_bias=forget_bias, w_ogate=w_ogate, w_out=w_out, w_gu=w_gu, w_down=w_down, gain_attn=gain_attn, gain_mlp=gain_mlp, qk_gain=qk_gain)


epsilon = 1e-06
highest = lax.Precision.HIGHEST

@jax.custom_vjp
def low(v):
    return lax.optimization_barrier(v.astype(jnp.bfloat16)).astype(jnp.float32)

@jax.custom_vjp
def low_back(v):
    return v

def low_keep(v):
    return (low(v), None)

def low_pass(kept, grad):
    return (grad,)

def back_keep(v):
    return (v, None)

def back_low(kept, grad):
    return (low(grad),)
low.defvjp(low_keep, low_pass)
low_back.defvjp(back_keep, back_low)

def norm_rows(values, gain):
    return values * lax.rsqrt(lax.optimization_barrier(jnp.mean(values * values, axis=-1, keepdims=True)) + epsilon) * gain

def attend_one(pieces):
    query_block, key_block, value_block, cum_block = pieces
    length = query_block.shape[0]
    score_raw = jnp.einsum('ie,je->ij', query_block, key_block, precision=highest) * query_block.shape[-1] ** (-0.5)
    score_raw = low_back(score_raw + cum_block[:, None] - cum_block[None, :])
    places = jnp.arange(length, dtype=jnp.int32)
    causal = places[None, :] <= places[:, None]
    masked = jnp.where(causal, score_raw, -jnp.inf)
    weights = jax.nn.softmax(masked, axis=-1)
    return jnp.einsum('ij,je->ie', low(weights), value_block, precision=highest)

def residual_block(inputs, w_qkv, w_forget, forget_bias, w_ogate, w_out, w_gu, w_down, gain_attn, gain_mlp, qk_gain, valid):
    groups, length, width = inputs.shape
    normed = low(norm_rows(inputs, gain_attn))
    qkv_rows = jnp.einsum('gld,dch->glch', normed, w_qkv, precision=highest)
    query_raw = low_back(qkv_rows[:, :, 0]).reshape(groups, length, HEADS, HEAD)
    key_raw = low_back(qkv_rows[:, :, 1]).reshape(groups, length, HEADS, HEAD)
    values_all = low(low_back(qkv_rows[:, :, 2])).reshape(groups, length, HEADS, HEAD)
    queries = low(norm_rows(query_raw, qk_gain[0]))
    keys_all = low(norm_rows(key_raw, qk_gain[1]))
    forget_pre = low_back(jnp.einsum('gld,dh->glh', normed, w_forget, precision=highest)) + forget_bias
    cum = jnp.cumsum(jax.nn.log_sigmoid(forget_pre), axis=1)

    def heads_first(values):
        return jnp.moveaxis(values, 2, 1).reshape(groups * HEADS, length, HEAD)
    pieces = (heads_first(queries), heads_first(keys_all), heads_first(values_all), jnp.moveaxis(cum, 2, 1).reshape(groups * HEADS, length))
    attended = lax.map(jax.checkpoint(attend_one), pieces)
    attended = jnp.moveaxis(attended.reshape(groups, HEADS, length, HEAD), 1, 2).reshape(groups, length, HEADS * HEAD)
    attended = low_back(attended)
    opener = jax.nn.sigmoid(low_back(jnp.einsum('gld,dh->glh', normed, w_ogate, precision=highest)))
    gated = low(attended * opener)
    branch = low_back(jnp.einsum('glh,dh->gld', gated, w_out, precision=highest))
    middle = inputs + branch
    normed_mid = low(norm_rows(middle, gain_mlp))
    both = low_back(jnp.einsum('gld,dcf->glcf', normed_mid, w_gu, precision=highest))
    hidden = low(jax.nn.silu(both[:, :, 0]) * both[:, :, 1])
    down = low_back(jnp.einsum('glf,df->gld', hidden, w_down, precision=highest))
    return valid[:, :, None] * (middle + down)

def reference(tokens, cotangent, lengths, w_qkv, w_forget, forget_bias, w_ogate, w_out, w_gu, w_down, gain_attn, gain_mlp, qk_gain):
    params = tuple((p.astype(jnp.float32) for p in (w_qkv, w_forget, forget_bias, w_ogate, w_out, w_gu, w_down, gain_attn, gain_mlp, qk_gain)))
    group_size = 4
    count = tokens.shape[0] // group_size
    inputs = tokens.astype(jnp.float32).reshape(count, group_size, LEN, D)
    cots = cotangent.astype(jnp.float32).reshape(count, group_size, LEN, D)
    lens = lengths.reshape(count, group_size)

    def one_group(totals, pieces):
        group_in, group_cot, group_len = pieces
        valid = (jnp.arange(LEN, dtype=jnp.int32)[None, :] < group_len[:, None]).astype(jnp.float32)

        def forward(first, *rest):
            return residual_block(first, *rest, valid)
        result, pullback = jax.vjp(forward, group_in, *params)
        grads = pullback(group_cot)
        new_totals = tuple((a + b for a, b in zip(totals, grads[1:])))
        return (new_totals, (result.astype(jnp.bfloat16), grads[0].astype(jnp.bfloat16)))
    zeros = tuple((jnp.zeros_like(p) for p in params))
    totals, (results, input_grads) = lax.scan(one_group, zeros, (inputs, cots, lens))
    return (results.reshape(tokens.shape), input_grads.reshape(tokens.shape), totals[0], totals[1], totals[2], totals[3], totals[4], totals[5], totals[6], totals[7], totals[8], totals[9])
```

```python
import functools
import math

import jax
import jax.numpy as jnp
from jax import lax
from jax.experimental import pallas as pl
from jax.experimental.pallas import tpu as pltpu
from jax.sharding import PartitionSpec as P

epsilon = 1e-06
f32 = jnp.float32
bf16 = jnp.bfloat16
BIG = 1e30
VMEM_LIMIT = 60 * 1024 * 1024


def mm(left, right):
    return jnp.dot(left, right, preferred_element_type=f32)


def mm_nt(left, right):
    return lax.dot_general(left, right, (((1,), (1,)), ((), ())), preferred_element_type=f32)


def mm_tn(left, right):
    return lax.dot_general(left, right, (((0,), (0,)), ((), ())), preferred_element_type=f32)


def whole(shape):
    return pl.BlockSpec(shape, lambda *_: (0,) * len(shape))


def call(kernel, outs, *operands, grid=None, in_specs=None, out_specs=None, scratch=(), flops=0):
    size = sum(math.prod(o.shape) * o.dtype.itemsize for o in list(operands) + list(outs))
    extra = {}
    if grid is not None:
        extra = dict(grid=grid, in_specs=in_specs, out_specs=out_specs)
    return pl.pallas_call(
        kernel,
        out_shape=outs,
        scratch_shapes=list(scratch),
        compiler_params=pltpu.CompilerParams(vmem_limit_bytes=VMEM_LIMIT),
        cost_estimate=pl.CostEstimate(flops=int(flops), bytes_accessed=int(size), transcendentals=0),
        **extra,
    )(*operands)


def sds(shape, dtype):
    return jax.ShapeDtypeStruct(shape, dtype)


def swap(value, axis, bit):
    n = lax.axis_size(axis)
    return lax.ppermute(value, axis, [(j, j ^ bit) for j in range(n)])


def gather_rows(own):
    n = lax.axis_size("tp")
    return [own] + [swap(own, "tp", k) for k in range(1, n)]


def scatter_rows(parts):
    n = lax.axis_size("tp")
    got = [swap(parts[k], "tp", k) for k in range(1, n)]
    total = parts[0].astype(f32)
    for g in got:
        total = total + g.astype(f32)
    return total


def sum_all(value):
    for axis in ("ctx", "tp", "shard"):
        n = lax.axis_size(axis)
        total = value
        for k in range(1, n):
            total = total + swap(value, axis, k)
        value = total
    return value


def project_kernel(heads, size, chunks, *refs):
    x_refs = refs[:chunks]
    w_ref, gain_ref, qk_ref, bias_ref, rank_ref, rank_t_ref = refs[chunks : chunks + 6]
    (normed_ref, q_ref, kv_ref, qraw_ref, kraw_ref, open_ref, pre_ref, cum_ref, cumt_ref) = refs[
        chunks + 6 :
    ]
    rows = x_refs[0].shape[0]
    cols = heads * size
    gain = gain_ref[...]
    for c in range(chunks):
        x = x_refs[c][...].astype(f32)
        r = lax.rsqrt(jnp.mean(x * x, axis=1, keepdims=True) + epsilon)
        normed_ref[c * rows : (c + 1) * rows, :] = (x * r * gain).astype(bf16)
    normed = normed_ref[...]
    for which, raw_ref, out_ref in ((0, qraw_ref, q_ref), (1, kraw_ref, kv_ref)):
        raw = mm(normed, w_ref[:, which * cols : (which + 1) * cols])
        raw_ref[...] = raw
        g = qk_ref[which : which + 1, :]
        for h in range(heads):
            piece = raw[:, h * size : (h + 1) * size]
            r = lax.rsqrt(jnp.mean(piece * piece, axis=1, keepdims=True) + epsilon)
            out_ref[:, h * size : (h + 1) * size] = (piece * r * g).astype(bf16)
    kv_ref[:, cols : 2 * cols] = mm(normed, w_ref[:, 2 * cols : 3 * cols]).astype(bf16)
    open_ref[...] = jax.nn.sigmoid(mm(normed, w_ref[:, 3 * cols : 4 * cols]))
    pre = mm(normed, w_ref[:, 4 * cols :]) + bias_ref[...]
    pre_ref[...] = pre
    logs = jnp.minimum(pre, 0.0) - jnp.log(1.0 + jnp.exp(-jnp.abs(pre)))
    earlier = (rank_t_ref[...] <= rank_ref[...]).astype(f32)
    cum = lax.dot_general(
        earlier, logs, (((1,), (0,)), ((), ())), precision=lax.Precision.HIGHEST, preferred_element_type=f32
    )
    total = jnp.sum(logs, axis=0, keepdims=True)
    cum_ref[...] = cum
    cumt_ref[0:8, :] = jnp.transpose(cum)[0:8, :]
    cumt_ref[8:16, :] = jnp.transpose(cum - total)[0:8, :]


def attend_kernel(heads, size, q_ref, kv_ref, kvl_ref, cum_ref, cumt_ref, left_ref, open_ref, rank_ref, rank_t_ref,
                  wout_ref, gated_ref, att_ref, lse_ref, *branch_refs):
    cols = heads * size
    rows = q_ref.shape[0]
    scale = 1.0 / math.sqrt(size)
    chunks = len(branch_refs)
    step = rows // chunks
    block = min(256, rows)
    keep = rank_t_ref[...] <= rank_ref[...]
    for b in range(rows // block):
        at = slice(b * block, (b + 1) * block)
        mask = keep[at, :]
        lses = []
        for h in range(heads):
            hs = slice(h * size, (h + 1) * size)
            vs = slice(cols + h * size, cols + (h + 1) * size)
            q = q_ref[at, hs]
            cq = cum_ref[at, h : h + 1]
            left = mm_nt(q, kvl_ref[:, hs]) * scale + (cq - left_ref[h : h + 1, :])
            right = mm_nt(q, kv_ref[:, hs]) * scale + (cq - cumt_ref[h : h + 1, :])
            el = jnp.exp(left)
            er = jnp.exp(jnp.where(mask, right, -BIG))
            total = jnp.sum(el, axis=1, keepdims=True) + jnp.sum(er, axis=1, keepdims=True)
            o = mm(el.astype(bf16), kvl_ref[:, vs]) + mm(er.astype(bf16), kv_ref[:, vs])
            att = o / total
            att_ref[at, hs] = att
            gated_ref[at, hs] = (att * open_ref[at, hs]).astype(bf16)
            lses.append(jnp.log(total))
        lse_ref[at, :] = jnp.concatenate(lses + [jnp.zeros((block, 128 - heads), f32)], axis=1)
    w = wout_ref[...]
    for c in range(chunks):
        at = slice(c * step, (c + 1) * step)
        branch_refs[c][...] = mm_nt(gated_ref[at, :], w).astype(bf16)


def ffn_kernel(steps, chunks, nm_ref, cot_ref, wg_ref, wu_ref, wd_ref, hid_ref, dg_ref, du_ref, *rest):
    p_refs = rest[:chunks]
    acc_ref = rest[chunks]
    j = pl.program_id(0)
    gate = mm(nm_ref[...], wg_ref[...])
    up = mm(nm_ref[...], wu_ref[...])
    dh = mm(cot_ref[...], wd_ref[...])
    sig = jax.nn.sigmoid(gate)
    act = gate * sig
    hid_ref[...] = (act * up).astype(bf16)
    dg = (dh * up * sig * (1.0 + gate * (1.0 - sig))).astype(bf16)
    du = (dh * act).astype(bf16)
    dg_ref[...] = dg
    du_ref[...] = du
    part = mm_nt(dg, wg_ref[...]) + mm_nt(du, wu_ref[...])

    @pl.when(j == 0)
    def _():
        acc_ref[...] = part

    @pl.when(j > 0)
    def _():
        acc_ref[...] += part

    @pl.when(j == steps - 1)
    def _():
        rows = acc_ref.shape[0] // chunks
        for c in range(chunks):
            p_refs[c][...] = acc_ref[c * rows : (c + 1) * rows, :].astype(bf16)


def attend_back_kernel(heads, size, q_ref, kv_ref, kvl_ref, cum_ref, cumt_ref, left_ref, open_ref, att_ref, lse_ref,
                       rank_ref, rank_t_ref, db_ref, wout_ref,
                       dq_ref, dkv_ref, back_ref, dopen_ref, dcum_ref, dleft_ref):
    cols = heads * size
    rows = q_ref.shape[0]
    scale = 1.0 / math.sqrt(size)
    block = min(256, rows)
    keep = rank_t_ref[...] <= rank_ref[...]
    ones = jnp.ones((block, 64), bf16)
    dcs, dls = [], []
    dg_all = mm(db_ref[...], wout_ref[...])
    op = open_ref[...]
    att_all = att_ref[...]
    dopen_ref[...] = (dg_all * att_all * op * (1.0 - op)).astype(bf16)
    da_all = (dg_all * op).astype(bf16)
    prod = da_all.astype(f32) * att_all
    for h in range(heads):
        hs = slice(h * size, (h + 1) * size)
        vs = slice(cols + h * size, cols + (h + 1) * size)
        kl, kr = kvl_ref[:, hs], kv_ref[:, hs]
        vl, vr = kvl_ref[:, vs], kv_ref[:, vs]
        sums = [None] * 6
        row_sums = []
        for b in range(rows // block):
            at = slice(b * block, (b + 1) * block)
            q = q_ref[at, hs]
            da = da_all[at, hs]
            delta = jnp.sum(prod[at, hs], axis=1, keepdims=True)
            cq = cum_ref[at, h : h + 1] - lse_ref[at, h : h + 1]
            pl_ = jnp.exp(mm_nt(q, kl) * scale + (cq - left_ref[h : h + 1, :]))
            right = mm_nt(q, kr) * scale + (cq - cumt_ref[h : h + 1, :])
            pr = jnp.exp(jnp.where(keep[at, :], right, -BIG))
            dsl = (pl_ * (mm_nt(da, vl) - delta)).astype(bf16)
            dsr = (pr * (mm_nt(da, vr) - delta)).astype(bf16)
            dq_ref[at, hs] = (mm(dsl, kl) + mm(dsr, kr)) * scale
            fl, fr = dsl.astype(f32), dsr.astype(f32)
            row_sums.append(jnp.sum(fl, axis=1, keepdims=True) + jnp.sum(fr, axis=1, keepdims=True))
            new = [
                mm_tn(dsl, q),
                mm_tn(dsr, q),
                mm_tn(pl_.astype(bf16), da),
                mm_tn(pr.astype(bf16), da),
                jnp.sum(fl, axis=0, keepdims=True),
                jnp.sum(fr, axis=0, keepdims=True),
            ]
            sums = [n if s is None else s + n for s, n in zip(sums, new)]
        back_ref[:, hs] = (sums[0] * scale).astype(bf16)
        dkv_ref[:, hs] = sums[1] * scale
        back_ref[:, vs] = sums[2].astype(bf16)
        dkv_ref[:, vs] = sums[3]
        rs = jnp.concatenate(row_sums, axis=0)
        dls.append(-sums[4])
        dcs.append((rs, -sums[5]))
    pad = 128 - heads
    rs_all = jnp.concatenate([d[0] for d in dcs] + [jnp.zeros((rows, pad), f32)], axis=1)
    rs_t = jnp.transpose(rs_all)
    for h in range(heads):
        dcum_ref[h : h + 1, :] = rs_t[h : h + 1, :] + dcs[h][1]
        dleft_ref[h : h + 1, :] = dls[h]
    for h in range(heads, 8):
        dcum_ref[h : h + 1, :] = jnp.zeros((1, rows), f32)
        dleft_ref[h : h + 1, :] = jnp.zeros((1, rows), f32)


def project_back_kernel(heads, size, chunks, *refs):
    x_refs = refs[:chunks]
    (w_ref, qk_ref, qraw_ref, kraw_ref, dq_ref, dkv_ref, back_ref, dopen_ref, dcum_ref, dleft_ref, extra_ref, pre_ref,
     rank_ref, rank_t_ref) = refs[chunks : chunks + 14]
    mixed_ref, bias_ref, gain_ref, qkg_ref = refs[chunks + 14 : chunks + 18]
    out_refs = refs[chunks + 18 :]
    cols = heads * size
    rows = x_refs[0].shape[0]
    for which, raw_ref in ((0, qraw_ref), (1, kraw_ref)):
        g = qk_ref[which : which + 1, :]
        total = jnp.zeros((1, size), f32)
        for h in range(heads):
            hs = slice(h * size, (h + 1) * size)
            d = dq_ref[:, hs] if which == 0 else dkv_ref[:, hs] + back_ref[:, hs].astype(f32)
            raw = raw_ref[:, hs]
            r = lax.rsqrt(jnp.mean(raw * raw, axis=1, keepdims=True) + epsilon)
            u = raw * r
            total = total + jnp.sum(d * u, axis=0, keepdims=True)
            e = d * g
            mixed_ref[:, which * cols + h * size : which * cols + (h + 1) * size] = (
                r * (e - u * jnp.mean(e * u, axis=1, keepdims=True))
            ).astype(bf16)
        qkg_ref[which : which + 1, :] = total
    mixed_ref[:, 2 * cols : 3 * cols] = (dkv_ref[:, cols:] + back_ref[:, cols:].astype(f32)).astype(bf16)
    mixed_ref[:, 3 * cols : 4 * cols] = dopen_ref[...]
    later = (rank_t_ref[...] <= rank_ref[...]).astype(f32)
    dcum = dcum_ref[...] + dleft_ref[...]
    dlog = lax.dot_general(
        dcum, later, (((1,), (0,)), ((), ())), precision=lax.Precision.HIGHEST, preferred_element_type=f32
    ) + extra_ref[:, 0:1]
    dlog = jnp.concatenate([dlog, jnp.zeros((120, dlog.shape[1]), f32)], axis=0)
    df = jnp.transpose(dlog) * jax.nn.sigmoid(-pre_ref[...])
    bias_ref[...] = jnp.sum(df, axis=0, keepdims=True)
    mixed_ref[:, 4 * cols :] = df.astype(bf16)
    gain = jnp.zeros((1, x_refs[0].shape[1]), f32)
    for c in range(chunks):
        at = slice(c * rows, (c + 1) * rows)
        dn = mm_nt(mixed_ref[at, :], w_ref[...])
        out_refs[c][...] = dn.astype(bf16)
        x = x_refs[c][...].astype(f32)
        r = lax.rsqrt(jnp.mean(x * x, axis=1, keepdims=True) + epsilon)
        gain = gain + jnp.sum(dn * (x * r), axis=0, keepdims=True)
    gain_ref[...] = gain


def body(tokens, cotangent, lengths, w_qkv, w_forget, forget_bias, w_ogate, w_out, w_gu, w_down, gain_attn, gain_mlp,
         qk_gain):
    slots, rows, width = tokens.shape
    assert slots == 1
    n = lax.axis_size("tp")
    me = lax.axis_index("tp")
    half = lax.axis_index("ctx")
    both = ("shard", "ctx")
    span = rows * n
    heads = w_forget.shape[1]
    size = qk_gain.shape[1]
    cols = heads * size
    units = w_down.shape[1]
    slab = w_qkv.shape[0]

    x_own = tokens[0]
    x_parts = gather_rows(x_own)

    own_pos = half * span + me * rows + jnp.arange(rows, dtype=jnp.int32)
    valid = (own_pos < lengths[0]).astype(f32)[:, None]
    cot_own = (cotangent[0].astype(f32) * valid).astype(bf16)
    cot_own, _ = lax.optimization_barrier((cot_own, x_parts))
    cot_parts = gather_rows(cot_own)

    order = jnp.concatenate([(me ^ k) * rows + jnp.arange(rows, dtype=jnp.int32) for k in range(n)])
    rank, rank_t = order[:, None], order[None, :]

    first = jnp.concatenate(
        [w_qkv.reshape(slab, 3 * cols), w_ogate, w_forget, jnp.zeros((slab, 128 - heads), bf16)], axis=1
    )
    w_first = lax.all_gather(first, both, axis=0, tiled=True)
    w_out_full = lax.all_gather(w_out, both, axis=0, tiled=True)
    w_gu_full = lax.all_gather(w_gu.reshape(slab, 2 * units), both, axis=0, tiled=True)
    w_down_full = lax.all_gather(w_down, both, axis=0, tiled=True)

    bias = lax.dynamic_slice_in_dim(forget_bias, me * heads, heads)
    bias = jnp.concatenate([bias, jnp.zeros((128 - heads,), f32)])[None, :]
    gain_a, gain_m = gain_attn[None, :], gain_mlp[None, :]

    wide = w_first.shape[1]
    normed, q, kv, qraw, kraw, opener, pre, cum, cumt = call(
        functools.partial(project_kernel, heads, size, n),
        [
            sds((span, width), bf16),
            sds((span, cols), bf16),
            sds((span, 2 * cols), bf16),
            sds((span, cols), f32),
            sds((span, cols), f32),
            sds((span, cols), f32),
            sds((span, 128), f32),
            sds((span, 128), f32),
            sds((16, span), f32),
        ],
        *x_parts, w_first, gain_a, qk_gain, bias, rank, rank_t,
        flops=2 * span * width * wide,
    )
    left_to_right = [(0, 1)]
    kv_left = lax.ppermute(kv, "ctx", left_to_right)
    cum_left = lax.ppermute(cumt[8:16], "ctx", left_to_right)
    cum_left = jnp.where(half == 0, BIG, cum_left)
    cum_rows = cumt[0:8]

    gated, attended, lse, *branch = call(
        functools.partial(attend_kernel, heads, size),
        [sds((span, cols), bf16), sds((span, cols), f32), sds((span, 128), f32)] + [sds((rows, width), bf16)] * n,
        q, kv, kv_left, cum, cum_rows, cum_left, opener, rank, rank_t, w_out_full,
        flops=2 * span * 2 * span * cols * 2 + 2 * span * cols * width,
    )
    x_f = x_own.astype(f32)
    middle = x_f + scatter_rows(branch)
    r2 = lax.rsqrt(jnp.mean(middle * middle, axis=1, keepdims=True) + epsilon)
    u2 = middle * r2
    nm_own = (u2 * gain_m).astype(bf16)
    nm = jnp.concatenate(gather_rows(nm_own), axis=0)
    cot = jnp.concatenate(cot_parts, axis=0)

    tile = min(256, units)
    steps = units // tile
    hidden, d_gate, d_up, *p_parts = call(
        functools.partial(ffn_kernel, steps, n),
        [sds((span, units), bf16)] * 3 + [sds((rows, width), bf16)] * n,
        nm, cot, w_gu_full, w_gu_full, w_down_full,
        grid=(steps,),
        in_specs=[
            whole((span, width)),
            whole((span, width)),
            pl.BlockSpec((width, tile), lambda j: (0, j)),
            pl.BlockSpec((width, tile), lambda j: (0, j + steps)),
            pl.BlockSpec((width, tile), lambda j: (0, j)),
        ],
        out_specs=[pl.BlockSpec((span, tile), lambda j: (0, j))] * 3 + [whole((rows, width))] * n,
        scratch=[pltpu.VMEM((span, width), f32)],
        flops=2 * span * width * units * 5,
    )
    d_nm = scatter_rows(p_parts)

    def reduce_weight(grad):
        return lax.psum_scatter(grad.astype(bf16), both, scatter_dimension=0, tiled=True).astype(f32)

    d_units = jnp.concatenate([d_gate, d_up], axis=1)
    grad_gu = reduce_weight(mm_tn(nm, d_units)).reshape(slab, 2, units)
    grad_down = reduce_weight(mm_tn(cot, hidden))

    e2 = d_nm * gain_m
    d_middle = valid * cotangent[0].astype(f32) + r2 * (e2 - u2 * jnp.mean(e2 * u2, axis=1, keepdims=True))
    gain_m_part = jnp.sum(d_nm * u2, axis=0)
    db_parts = gather_rows(d_middle.astype(bf16))
    d_branch = jnp.concatenate(db_parts, axis=0)

    hidden_late, _ = lax.optimization_barrier((hidden, d_branch))
    down = mm_nt(hidden_late, w_down_full).astype(bf16)
    down_parts = [down[k * rows : (k + 1) * rows] for k in range(n)]
    output = (valid * (middle + scatter_rows(down_parts))).astype(bf16)

    grad_out = reduce_weight(mm_tn(d_branch, gated))
    dq, dkv, back, d_open, d_cum, d_left = call(
        functools.partial(attend_back_kernel, heads, size),
        [
            sds((span, cols), f32),
            sds((span, 2 * cols), f32),
            sds((span, 2 * cols), bf16),
            sds((span, cols), bf16),
            sds((8, span), f32),
            sds((8, span), f32),
        ],
        q, kv, kv_left, cum, cum_rows, cum_left, opener, attended, lse, rank, rank_t, d_branch, w_out_full,
        flops=2 * span * 2 * span * cols * 5 + 2 * span * cols * width,
    )
    right_to_left = [(1, 0)]
    back = lax.ppermute(back, "ctx", right_to_left)
    sent = jnp.concatenate([d_left, jnp.broadcast_to(jnp.sum(d_cum, axis=1, keepdims=True), (8, 128))], axis=1)
    sent = lax.ppermute(sent, "ctx", right_to_left)
    d_left, extra = sent[:, :span], sent[:, span:]

    mixed, bias_part, gain_part, qkg_part, *dn_parts = call(
        functools.partial(project_back_kernel, heads, size, n),
        [sds((span, wide), bf16), sds((1, 128), f32), sds((1, width), f32), sds((2, size), f32)]
        + [sds((rows, width), bf16)] * n,
        *x_parts, w_first, qk_gain, qraw, kraw, dq, dkv, back, d_open, d_cum, d_left, extra, pre, rank, rank_t,
        flops=2 * span * width * wide,
    )
    d_normed = scatter_rows(dn_parts)
    grad_first = reduce_weight(mm_tn(normed, mixed))
    grad_qkv = grad_first[:, : 3 * cols].reshape(slab, 3, cols)
    grad_ogate = grad_first[:, 3 * cols : 4 * cols]
    grad_forget = grad_first[:, 4 * cols : 4 * cols + heads]

    r1 = lax.rsqrt(jnp.mean(x_f * x_f, axis=1, keepdims=True) + epsilon)
    u1 = x_f * r1
    e1 = d_normed * gain_a
    input_grad = (d_middle + r1 * (e1 - u1 * jnp.mean(e1 * u1, axis=1, keepdims=True))).astype(bf16)

    bias_full = lax.dynamic_update_slice_in_dim(
        jnp.zeros(forget_bias.shape, f32), bias_part[0, :heads], me * heads, 0
    )
    small = sum_all(jnp.concatenate([gain_part[0], gain_m_part, qkg_part.reshape(-1), bias_full]))
    edges = [0, width, 2 * width, 2 * width + 2 * size]
    return (
        output[None],
        input_grad[None],
        grad_qkv,
        grad_forget,
        small[edges[3] :],
        grad_ogate,
        grad_out,
        grad_gu,
        grad_down,
        small[edges[0] : edges[1]],
        small[edges[1] : edges[2]],
        small[edges[2] : edges[3]].reshape(2, size),
    )


def solution(mesh):
    rows = P("shard", ("ctx", "tp"), None)
    flat = P(("shard", "ctx"), "tp")
    deep = P(("shard", "ctx"), None, "tp")
    return jax.shard_map(
        body,
        mesh=mesh,
        in_specs=(rows, rows, P("shard"), deep, flat, P(), flat, flat, deep, flat, P(), P(), P()),
        out_specs=(rows, rows, deep, flat, P(), flat, flat, deep, flat, P(), P(), P()),
        check_vma=False,
    )
```

```python
import functools
import math

import jax
import jax.numpy as jnp
from jax import lax
from jax.experimental import pallas as pl
from jax.experimental.pallas import tpu as pltpu
from jax.sharding import PartitionSpec as P

epsilon = 1e-06
f32 = jnp.float32
bf16 = jnp.bfloat16
BIG = 1e30
VMEM_LIMIT = 60 * 1024 * 1024


def mm(left, right):
    return jnp.dot(left, right, preferred_element_type=f32)


def mm_nt(left, right):
    return lax.dot_general(left, right, (((1,), (1,)), ((), ())), preferred_element_type=f32)


def mm_tn(left, right):
    return lax.dot_general(left, right, (((0,), (0,)), ((), ())), preferred_element_type=f32)


def whole(shape):
    return pl.BlockSpec(shape, lambda *_: (0,) * len(shape))


def call(kernel, outs, *operands, grid=None, in_specs=None, out_specs=None, scratch=(), blocks=None, places=None,
         weight=0.1):
    extra = {}
    if grid is None and blocks:
        grid = (1,)
        places = places or {}
        in_specs = [
            pl.BlockSpec(blocks.get(i, o.shape), functools.partial(lambda at, *_: at, places.get(i, (0,) * o.ndim)))
            for i, o in enumerate(operands)
        ]
        out_specs = [whole(o.shape) for o in outs]
    if grid is not None:
        extra = dict(grid=grid, in_specs=in_specs, out_specs=out_specs)
    return pl.pallas_call(
        kernel,
        out_shape=outs,
        scratch_shapes=list(scratch),
        compiler_params=pltpu.CompilerParams(vmem_limit_bytes=VMEM_LIMIT),
        cost_estimate=pl.CostEstimate(flops=int(weight * 1e9), bytes_accessed=int(weight * 1e6), transcendentals=0),
        **extra,
    )(*operands)


def sds(shape, dtype):
    return jax.ShapeDtypeStruct(shape, dtype)


def swap(value, axis, bit):
    n = lax.axis_size(axis)
    return lax.ppermute(value, axis, [(j, j ^ bit) for j in range(n)])


def gather_rows(own):
    n = lax.axis_size("tp")
    return [own] + [swap(own, "tp", k) for k in range(1, n)]


def send_rows(parts):
    n = lax.axis_size("tp")
    return [parts[0]] + [swap(parts[k], "tp", k) for k in range(1, n)]


def gather_all(own):
    n = lax.axis_size("tp")
    return lax.all_to_all(jnp.broadcast_to(own[None], (n,) + own.shape), "tp", 0, 0, tiled=True)


def after(value, *others):
    return lax.optimization_barrier((value, others))[0]


def pick(value, index, axis=0):
    return lax.dynamic_index_in_dim(value, index, axis, keepdims=False)


def scatter_weight(part):
    shards, halves = lax.axis_size("shard"), lax.axis_size("ctx")
    me, half = lax.axis_index("shard"), lax.axis_index("ctx")
    width, cols = part.shape
    blocks = part.reshape(shards, halves, width // (shards * halves), cols)
    got = swap(pick(blocks, 1 - half, 1), "ctx", 1)
    keep = pick(blocks, half, 1)

    def pair(k):
        return pick(keep, me ^ k).astype(f32) + pick(got, me ^ k).astype(f32)

    arrived = [swap(pair(k).astype(bf16), "shard", k) for k in range(1, shards)]
    return pair(0), arrived


def finish_weight(state):
    own, arrived = state
    for g in arrived:
        own = own + g.astype(f32)
    return own


def sum_over(value, axes):
    for axis in axes:
        n = lax.axis_size(axis)
        total = value
        for k in range(1, n):
            total = total + swap(value, axis, k)
        value = total
    return value


def thirds(value):
    high = value.astype(bf16)
    rest = value - high.astype(f32)
    middle = rest.astype(bf16)
    return high, middle, (rest - middle.astype(f32)).astype(bf16)


def head_sums(value, size):
    cols = value.shape[1]
    shape = (cols, cols)
    row = lax.broadcasted_iota(jnp.int32, shape, 0) // size
    col = lax.broadcasted_iota(jnp.int32, shape, 1) // size
    same = (row == col).astype(bf16)
    high = value.astype(bf16)
    low = (value - high.astype(f32)).astype(bf16)
    return mm(high, same) + mm(low, same)


def spread(pieces, rows):
    used = sum(p.shape[1] for p in pieces)
    return jnp.concatenate(list(pieces) + [jnp.zeros((rows, 128 - used), bf16)], axis=1)


def running(mask, value, heads):
    rows = value.shape[0]
    parts = thirds(value[:, :heads])
    total = mm(mask, spread(parts, rows))
    return total[:, :heads] + total[:, heads : 2 * heads] + total[:, 2 * heads : 3 * heads]


def project_kernel(heads, size, chunks, *refs):
    x_refs, refs = refs[:chunks], refs[chunks:]
    w_ref, gain_ref, qk_ref, bias_ref, rank_ref, rank_t_ref = refs[:6]
    (normed_ref, qa_ref, ka_ref, va_ref, send_ref, qraw_ref, kraw_ref, open_ref, pre_ref, cum_ref) = refs[6:]
    rows = x_refs[0].shape[0]
    span = rows * chunks
    cols = heads * size
    gain = gain_ref[...]
    for c in range(chunks):
        x = x_refs[c][...].astype(f32)
        r = lax.rsqrt(jnp.mean(x * x, axis=1, keepdims=True) + epsilon)
        normed_ref[c * rows : (c + 1) * rows, :] = (x * r * gain).astype(bf16)
    normed = normed_ref[...]
    pre = mm(normed, w_ref[:, 4 * cols : 4 * cols + 128]) + bias_ref[...]
    pre_ref[...] = pre
    logs = jnp.minimum(pre, 0.0) - jnp.log(1.0 + jnp.exp(-jnp.abs(pre)))
    earlier = (rank_t_ref[...] <= rank_ref[...]).astype(bf16)
    cum = running(earlier, logs, heads)
    cum_ref[...] = jnp.concatenate([cum, jnp.zeros((span, 128 - heads), f32)], axis=1)
    ones = jnp.ones((span, 3), bf16)
    fill = jnp.zeros((span, 128 - size - 6), bf16)
    cums = thirds(cum)
    outs = thirds(-cum)
    fars = thirds(jnp.sum(logs[:, :heads], axis=0, keepdims=True) - cum)

    def at(parts, h):
        return [p[:, h : h + 1] for p in parts]

    for which, raw_ref in ((0, qraw_ref), (1, kraw_ref)):
        raw = mm(normed, w_ref[:, (which + 1) * cols : (which + 2) * cols])
        raw_ref[...] = raw
        r = lax.rsqrt(head_sums(raw * raw, size) * (1.0 / size) + epsilon)
        value = (raw * r * qk_ref[which : which + 1, :]).astype(bf16)
        if which == 0:
            value = value * jnp.asarray(1.0 / math.sqrt(size), bf16)
            for h in range(heads):
                piece = value[:, h * size : (h + 1) * size]
                qa_ref[:, h * 128 : (h + 1) * 128] = jnp.concatenate([piece] + at(cums, h) + [ones, fill], axis=1)
        else:
            send_ref[:, 0:cols] = value
            for h in range(heads):
                piece = value[:, h * size : (h + 1) * size]
                ka_ref[:, h * 128 : (h + 1) * 128] = jnp.concatenate([piece, ones] + at(outs, h) + [fill], axis=1)
    value = mm(normed, w_ref[:, 3 * cols : 4 * cols]).astype(bf16)
    send_ref[:, cols : 2 * cols] = value
    tail = jnp.concatenate([ones, jnp.zeros((span, 128 - size - 3), bf16)], axis=1)
    for h in range(heads):
        va_ref[:, h * 128 : (h + 1) * 128] = jnp.concatenate([value[:, h * size : (h + 1) * size], tail], axis=1)
    send_ref[:, 2 * cols :] = spread(fars, span)
    open_ref[...] = jax.nn.sigmoid(mm(normed, w_ref[:, 4 * cols + 128 :]))


def attend_kernel(heads, size, qa_ref, ka_ref, va_ref, left_ref, open_ref, rank_ref, rank_t_ref, wout_ref,
                  gated_ref, att_ref, lse_ref, kl_ref, vl_ref, *branch_refs):
    cols = heads * size
    rows = qa_ref.shape[0]
    chunks = len(branch_refs)
    step = rows // chunks
    keep = rank_t_ref[...] <= rank_ref[...]
    shut = jnp.where(lax.axis_index("ctx") == 0, -BIG, 0.0).astype(bf16)
    ones = jnp.ones((rows, 3), bf16)
    fill = jnp.zeros((rows, 128 - size - 6), bf16)
    tail = jnp.zeros((rows, 128 - size - 3), bf16)
    lses = []
    for h in range(heads):
        wide = slice(h * 128, (h + 1) * 128)
        hs = slice(h * size, (h + 1) * size)
        far = [left_ref[:, 2 * cols + i * heads + h : 2 * cols + i * heads + h + 1] for i in range(3)]
        kl = jnp.concatenate([left_ref[:, hs], ones, far[0] + shut, far[1], far[2], fill], axis=1)
        vl = jnp.concatenate([left_ref[:, cols + h * size : cols + (h + 1) * size], ones, tail], axis=1)
        kl_ref[:, wide] = kl
        vl_ref[:, wide] = vl
        q = qa_ref[:, wide]
        el = jnp.exp(mm_nt(q, kl)).astype(bf16)
        er = jnp.exp(jnp.where(keep, mm_nt(q, ka_ref[:, wide]), -BIG)).astype(bf16)
        o = mm(el, vl) + mm(er, va_ref[:, wide])
        total = o[:, size : size + 1]
        att = o[:, :size] / total
        att_ref[:, hs] = att
        gated_ref[:, hs] = (att * open_ref[:, hs]).astype(bf16)
        lses.append(jnp.log(total))
    lse_ref[...] = jnp.concatenate(lses + [jnp.zeros((rows, 128 - heads), f32)], axis=1)
    branch = mm_nt(gated_ref[...], wout_ref[...]).astype(bf16)
    for c in range(chunks):
        branch_refs[c][...] = branch[c * step : (c + 1) * step, :]


def hidden_back_kernel(chunks, cot_ref, wd_ref, dh_ref, order_ref):
    me = lax.axis_index("tp")
    rows = cot_ref.shape[1]

    @pl.when(pl.program_id(0) == 0)
    def _():
        for c in range(chunks):
            order_ref[c * rows : (c + 1) * rows, :] = cot_ref[pl.ds(me ^ c, 1)][0]

    dh_ref[...] = mm(order_ref[...], wd_ref[...])


def ffn_kernel(steps, chunks, *refs):
    nm_refs, refs = refs[:chunks], refs[chunks:]
    dh_ref, wg_ref, wu_ref, nm_ref, hid_ref, dgu_ref = refs[:6]
    p_refs, refs = refs[6 : 6 + chunks], refs[6 + chunks :]
    w_all = refs[0]
    rows = nm_refs[0].shape[0]
    tile = wg_ref.shape[1]
    units = tile * steps
    j = pl.program_id(0)

    @pl.when(j == 0)
    def _():
        for c in range(chunks):
            nm_ref[c * rows : (c + 1) * rows, :] = nm_refs[c][...]

    gate = mm(nm_ref[...], wg_ref[...])
    up = mm(nm_ref[...], wu_ref[...])
    dh = dh_ref[...]
    sig = jax.nn.sigmoid(gate)
    act = gate * sig
    hid_ref[...] = (act * up).astype(bf16)
    dg = (dh * up * sig * (1.0 + gate * (1.0 - sig))).astype(bf16)
    du = (dh * act).astype(bf16)
    for s in range(steps):

        @pl.when(j == s)
        def _():
            at, up_at = slice(s * tile, (s + 1) * tile), slice(units + s * tile, units + (s + 1) * tile)
            dgu_ref[:, at] = dg
            dgu_ref[:, up_at] = du
            w_all[:, at] = wg_ref[...]
            w_all[:, up_at] = wu_ref[...]

    @pl.when(j == steps - 1)
    def _():
        width = w_all.shape[0]
        for b in range(0, width, 256):
            part = mm_nt(dgu_ref[...], w_all[b : b + 256, :]).astype(bf16)
            for c in range(chunks):
                p_refs[c][:, b : b + 256] = part[c * rows : (c + 1) * rows, :]


def down_kernel(chunks, hid_ref, wd_ref, out_ref):
    me = lax.axis_index("tp")
    down = mm_nt(hid_ref[...], wd_ref[...]).astype(bf16)
    rows = out_ref.shape[1]
    for c in range(chunks):
        out_ref[pl.ds(me ^ c, 1)] = down[c * rows : (c + 1) * rows, :][None]


def attend_back_kernel(heads, size, chunks, *refs):
    db_refs, refs = refs[:chunks], refs[chunks:]
    (qa_ref, ka_ref, va_ref, kl_ref, vl_ref, cum_ref, lse_ref, open_ref, att_ref, rank_ref, rank_t_ref,
     wout_ref) = refs[:12]
    branch_ref, dq_ref, dk_ref, dv_ref, back_ref, dopen_ref, dcum_ref = refs[12:]
    cols = heads * size
    part = db_refs[0].shape[0]
    rows = part * chunks
    for c in range(chunks):
        branch_ref[c * part : (c + 1) * part, :] = db_refs[c][...]
    keep = rank_t_ref[...] >= rank_ref[...]
    dg = mm(branch_ref[...], wout_ref[...])
    op = open_ref[...]
    att = att_ref[...]
    dopen_ref[...] = (dg * att * op * (1.0 - op)).astype(bf16)
    da_all = (dg * op).astype(bf16)
    prod = da_all.astype(f32) * att
    place = thirds(cum_ref[:, :heads] - lse_ref[:, :heads])
    ones = jnp.ones((rows, 3), bf16)
    fill = jnp.zeros((rows, 128 - size - 6), bf16)
    tail = jnp.zeros((rows, 128 - size - 3), bf16)
    owns, lefts = [], []
    for h in range(heads):
        wide = slice(h * 128, (h + 1) * 128)
        hs = slice(h * size, (h + 1) * size)
        vs = slice(cols + h * size, cols + (h + 1) * size)
        q = jnp.concatenate([qa_ref[:, h * 128 : h * 128 + size]] + [p[:, h : h + 1] for p in place] + [ones, fill], axis=1)
        delta = thirds(-jnp.sum(prod[:, hs], axis=1, keepdims=True))
        da = jnp.concatenate([da_all[:, hs], delta[0], delta[1], delta[2], tail], axis=1)
        dq = jnp.zeros((rows, 128), f32)
        found = []
        for k_ref, v_ref, right in ((kl_ref, vl_ref, False), (ka_ref, va_ref, True)):
            k, v = k_ref[:, wide], v_ref[:, wide]
            score = mm_nt(k, q)
            if right:
                score = jnp.where(keep, score, -BIG)
            p = jnp.exp(score)
            ds = (p * mm_nt(v, da)).astype(bf16)
            found += [mm(p.astype(bf16), da)[:, :size], mm(ds, q)]
            dq = dq + mm_tn(ds, k)
        dq_ref[:, hs] = dq[:, :size] * (1.0 / math.sqrt(size))
        back_ref[:, vs] = found[0].astype(bf16)
        back_ref[:, hs] = found[1][:, :size].astype(bf16)
        dv_ref[:, hs] = found[2]
        dk_ref[:, hs] = found[3][:, :size]
        lefts.append(-found[1][:, size + 3 : size + 4])
        owns.append(dq[:, size : size + 1] - found[3][:, size + 3 : size + 4])
    own = jnp.concatenate(owns, axis=1)
    dcum_ref[...] = jnp.concatenate([own, jnp.zeros((rows, 128 - heads), f32)], axis=1)
    total = jnp.broadcast_to(jnp.sum(own, axis=0, keepdims=True), (rows, heads))
    sent = thirds(jnp.concatenate(lefts, axis=1)) + thirds(total)
    back_ref[:, 2 * cols :] = spread(sent, rows)


def project_back_kernel(heads, size, chunks, *refs):
    x_refs, refs = refs[:chunks], refs[chunks:]
    (w_ref, qk_ref, qraw_ref, kraw_ref, dq_ref, dk_ref, dv_ref, back_ref, dopen_ref, dcum_ref, pre_ref, rank_ref,
     rank_t_ref, gm_ref) = refs[:14]
    mixed_ref, out_refs = refs[14], refs[15:]
    cols = heads * size
    width = x_refs[0].shape[1]
    rows = x_refs[0].shape[0]
    span = rows * chunks
    sums = []
    for which, raw_ref in ((0, qraw_ref), (1, kraw_ref)):
        d = dq_ref[...] if which == 0 else dk_ref[...] + back_ref[:, :cols].astype(f32)
        raw = raw_ref[...]
        r = lax.rsqrt(head_sums(raw * raw, size) * (1.0 / size) + epsilon)
        u = raw * r
        total = jnp.sum(d * u, axis=0, keepdims=True)
        sums.append(sum(total[:, h * size : (h + 1) * size] for h in range(heads)))
        e = d * qk_ref[which : which + 1, :]
        mixed_ref[:, which * cols : (which + 1) * cols] = (
            r * (e - u * (head_sums(e * u, size) * (1.0 / size)))
        ).astype(bf16)
    mixed_ref[:, 2 * cols : 3 * cols] = (dv_ref[...] + back_ref[:, cols : 2 * cols].astype(f32)).astype(bf16)
    mixed_ref[:, 3 * cols + 128 :] = dopen_ref[...]
    extra = back_ref[:, 2 * cols :].astype(f32)
    got = extra[:, :heads] + extra[:, heads : 2 * heads] + extra[:, 2 * heads : 3 * heads]
    after_sum = extra[:, 3 * heads : 4 * heads] + extra[:, 4 * heads : 5 * heads] + extra[:, 5 * heads : 6 * heads]
    later = (rank_t_ref[...] >= rank_ref[...]).astype(bf16)
    dlog = running(later, dcum_ref[:, :heads] + got, heads) + after_sum
    df = jnp.concatenate([dlog, jnp.zeros((span, 128 - heads), f32)], axis=1) * jax.nn.sigmoid(-pre_ref[...])
    bias = jnp.sum(df, axis=0, keepdims=True)
    mixed_ref[:, 3 * cols : 3 * cols + 128] = df.astype(bf16)
    gain = jnp.zeros((1, width), f32)
    lows = []
    for c in range(chunks):
        at = slice(c * rows, (c + 1) * rows)
        dn = mm_nt(mixed_ref[at, :], w_ref[:, cols:])
        out_refs[c][0:rows, :] = dn.astype(bf16)
        x = x_refs[c][...].astype(f32)
        r = lax.rsqrt(jnp.mean(x * x, axis=1, keepdims=True) + epsilon)
        gain = gain + jnp.sum(dn * (x * r), axis=0, keepdims=True)
    lanes = jnp.concatenate([sums[0], sums[1], bias, jnp.zeros((1, width - 2 * size - 128), f32)], axis=1)
    low = jnp.concatenate([gain, lanes, gm_ref[...], jnp.zeros((13, width), f32)], axis=0).astype(bf16)
    for c in range(chunks):
        out_refs[c][rows : rows + 16, :] = low


def middle_kernel(chunks, x_ref, gain_ref, *refs):
    middle = x_ref[...].astype(f32)
    for c in range(chunks):
        middle = middle + refs[c][...].astype(f32)
    mid_ref, nm_ref = refs[chunks:]
    mid_ref[...] = middle
    r = lax.rsqrt(jnp.mean(middle * middle, axis=1, keepdims=True) + epsilon)
    nm_ref[...] = (middle * r * gain_ref[...]).astype(bf16)


def norm_back(d, v, gain):
    r = lax.rsqrt(jnp.mean(v * v, axis=1, keepdims=True) + epsilon)
    u = v * r
    e = d * gain
    return r * (e - u * jnp.mean(e * u, axis=1, keepdims=True)), jnp.sum(d * u, axis=0, keepdims=True)


def middle_back_kernel(chunks, mid_ref, cot_ref, gain_ref, *refs):
    d = refs[0][...].astype(f32)
    for c in range(1, chunks):
        d = d + refs[c][...].astype(f32)
    dmid_ref, branch_ref, part_ref = refs[chunks:]
    back, part = norm_back(d, mid_ref[...], gain_ref[...])
    back = back + cot_ref[...].astype(f32)
    dmid_ref[...] = back
    branch_ref[...] = back.astype(bf16)
    part_ref[...] = part


def input_back_kernel(chunks, x_ref, dmid_ref, gain_ref, *refs):
    rows = x_ref.shape[0]
    d = refs[0][...].astype(f32)
    for c in range(1, chunks):
        d = d + refs[c][...].astype(f32)
    back, _ = norm_back(d[0:rows, :], x_ref[...].astype(f32), gain_ref[...])
    refs[chunks][...] = (back + dmid_ref[...]).astype(bf16)
    refs[chunks + 1][...] = d[rows:, :]


def body(tokens, cotangent, lengths, w_qkv, w_forget, forget_bias, w_ogate, w_out, w_gu, w_down, gain_attn, gain_mlp,
         qk_gain):
    slots, rows, width = tokens.shape
    assert slots == 1
    n = lax.axis_size("tp")
    me = lax.axis_index("tp")
    half = lax.axis_index("ctx")
    both = ("shard", "ctx")
    span = rows * n
    heads = w_forget.shape[1]
    size = qk_gain.shape[1]
    cols = heads * size
    units = w_down.shape[1]
    slab = w_qkv.shape[0]

    x_own = tokens[0]
    x_parts = gather_rows(x_own)

    own_pos = half * span + me * rows + jnp.arange(rows, dtype=jnp.int32)
    valid = (own_pos < lengths[0]).astype(f32)[:, None]
    cot_own = (cotangent[0].astype(f32) * valid).astype(bf16)
    cot = gather_all(after(cot_own, *x_parts))

    order = jnp.concatenate([(me ^ k) * rows + jnp.arange(rows, dtype=jnp.int32) for k in range(n)])
    rank, rank_t = order[:, None], order[None, :]

    first = jnp.concatenate(
        [w_out, w_qkv.reshape(slab, 3 * cols), w_forget, jnp.zeros((slab, 128 - heads), bf16), w_ogate], axis=1
    )
    first = lax.all_gather(first, both, axis=0, tiled=True)
    rest = jnp.concatenate([w_gu.reshape(slab, 2 * units), w_down], axis=1)
    rest = lax.all_gather(rest, both, axis=0, tiled=True)
    wide = 4 * cols + 128
    w_out_full, out_block = first, (width, cols)
    if cols % 128:
        w_out_full = first[:, :cols]

    bias = lax.dynamic_slice_in_dim(forget_bias, me * heads, heads)
    bias = jnp.concatenate([bias, jnp.zeros((128 - heads,), f32)])[None, :]
    gain_a, gain_m = gain_attn[None, :], gain_mlp[None, :]
    qk_wide = jnp.tile(qk_gain, (1, heads))

    normed, qa, ka, va, sent, qraw, kraw, opener, pre, cum = call(
        functools.partial(project_kernel, heads, size, n),
        [
            sds((span, width), bf16),
            sds((span, heads * 128), bf16),
            sds((span, heads * 128), bf16),
            sds((span, heads * 128), bf16),
            sds((span, 2 * cols + 128), bf16),
            sds((span, cols), f32),
            sds((span, cols), f32),
            sds((span, cols), f32),
            sds((span, 128), f32),
            sds((span, 128), f32),
        ],
        *x_parts, first, gain_a, qk_wide, bias, rank, rank_t,
    )
    left = lax.ppermute(sent, "ctx", [(0, 1)])
    gated, attended, lse, kl, vl, *branch = call(
        functools.partial(attend_kernel, heads, size),
        [sds((span, cols), bf16), sds((span, cols), f32), sds((span, 128), f32)]
        + [sds((span, heads * 128), bf16)] * 2
        + [sds((rows, width), bf16)] * n,
        qa, ka, va, left, opener, rank, rank_t, w_out_full,
        blocks={7: out_block},
    )
    tile = min(512, units)
    steps = units // tile
    d_hidden, cot = call(
        functools.partial(hidden_back_kernel, n),
        [sds((span, units), f32), sds((span, width), bf16)],
        after(cot, branch), rest,
        grid=(steps,),
        in_specs=[whole((n, rows, width)), pl.BlockSpec((width, tile), lambda j: (0, j + 2 * steps))],
        out_specs=[pl.BlockSpec((span, tile), lambda j: (0, j)), whole((span, width))],
    )
    middle, nm_own = call(
        functools.partial(middle_kernel, n),
        [sds((rows, width), f32), sds((rows, width), bf16)],
        x_own, gain_m, *send_rows(branch),
    )
    nm_parts = after(gather_rows(nm_own), d_hidden)
    nm, hidden, d_units, *p_parts = call(
        functools.partial(ffn_kernel, steps, n),
        [sds((span, width), bf16), sds((span, units), bf16), sds((span, 2 * units), bf16)]
        + [sds((rows, width), bf16)] * n,
        *nm_parts, d_hidden, rest, rest,
        grid=(steps,),
        in_specs=[whole((rows, width))] * n
        + [
            pl.BlockSpec((span, tile), lambda j: (0, j)),
            pl.BlockSpec((width, tile), lambda j: (0, j)),
            pl.BlockSpec((width, tile), lambda j: (0, j + steps)),
        ],
        out_specs=[whole((span, width)), pl.BlockSpec((span, tile), lambda j: (0, j)), whole((span, 2 * units))]
        + [whole((rows, width))] * n,
        scratch=[pltpu.VMEM((width, 2 * units), bf16)],
    )
    p_got = send_rows(p_parts)
    part_ffn = jnp.concatenate([mm_tn(nm, d_units).astype(bf16), mm_tn(cot, hidden).astype(bf16)], axis=1)
    grad_ffn = lax.psum_scatter(after(part_ffn, *p_got), both, scatter_dimension=0, tiled=True)
    d_middle, db_own, gain_m_part = call(
        functools.partial(middle_back_kernel, n),
        [sds((rows, width), f32), sds((rows, width), bf16), sds((1, width), f32)],
        middle, cot_own, gain_m, *after(p_got, part_ffn),
    )
    db_parts = gather_rows(db_own)
    (down,) = call(
        functools.partial(down_kernel, n),
        [sds((n, rows, width), bf16)],
        after(hidden, db_own), rest,
        blocks={1: (width, units)}, places={1: (0, 2)},
    )
    down = lax.all_to_all(after(down, db_parts), "tp", 0, 0, tiled=True)
    down_sum = jnp.sum(down.astype(f32), axis=0)
    output = (valid * (middle + down_sum)).astype(bf16)

    d_branch, dq, dk, dv, back, d_open, d_cum = call(
        functools.partial(attend_back_kernel, heads, size, n),
        [
            sds((span, width), bf16),
            sds((span, cols), f32),
            sds((span, cols), f32),
            sds((span, cols), f32),
            sds((span, 2 * cols + 128), bf16),
            sds((span, cols), bf16),
            sds((span, 128), f32),
        ],
        *db_parts, qa, ka, va, kl, vl, cum, lse, opener, attended, rank, rank_t, w_out_full,
        blocks={n + 11: out_block}, weight=100,
    )
    part_gates = jnp.concatenate([mm_tn(d_branch, gated), mm_tn(normed, d_open)], axis=1).astype(bf16)
    grad_gates = lax.psum_scatter(after(part_gates, grad_ffn), both, scatter_dimension=0, tiled=True)
    back = lax.ppermute(back, "ctx", [(1, 0)])
    mixed, *dn = call(
        functools.partial(project_back_kernel, heads, size, n),
        [sds((span, wide), bf16)] + [sds((rows + 16, width), bf16)] * n,
        *x_parts, first, qk_wide, qraw, kraw, dq, dk, dv, back, d_open, d_cum, pre, rank, rank_t, gain_m_part,
    )
    deep = 3 * cols + 128
    dn = send_rows(dn)
    state_qkv = scatter_weight(mm_tn(normed, mixed[:, :deep]).astype(bf16))
    input_grad, own_sums = call(
        functools.partial(input_back_kernel, n),
        [sds((rows, width), bf16), sds((16, width), f32)],
        x_own, d_middle, gain_a, *after(dn, grad_gates, output, state_qkv[1]),
    )
    grad_ffn, grad_gates = grad_ffn.astype(f32), grad_gates.astype(f32)
    grad_gu, grad_down = grad_ffn[:, : 2 * units].reshape(slab, 2, units), grad_ffn[:, 2 * units :]
    grad_out, grad_ogate = grad_gates[:, :cols], grad_gates[:, cols:]
    grad_first = finish_weight(state_qkv)
    grad_qkv = grad_first[:, : 3 * cols].reshape(slab, 3, cols)
    grad_forget = grad_first[:, 3 * cols : 3 * cols + heads]

    me_bits = [(me ^ k) * heads for k in range(n)]
    bias_sum = jnp.zeros((n * heads,), f32)
    for k in range(n):
        bias_sum = lax.dynamic_update_slice_in_dim(
            bias_sum, dn[k][rows + 1, 2 * size : 2 * size + heads].astype(f32), me_bits[k], 0
        )
    small = jnp.concatenate([own_sums[0], own_sums[1, : 2 * size], bias_sum, own_sums[2]])
    small = sum_over(small, ("ctx", "shard"))
    edges = [0, width, width + 2 * size, width + 2 * size + n * heads]
    return (
        output[None],
        input_grad[None],
        grad_qkv,
        grad_forget,
        small[edges[2] : edges[3]],
        grad_ogate,
        grad_out,
        grad_gu,
        grad_down,
        small[edges[0] : edges[1]],
        small[edges[2] + n * heads :],
        small[edges[1] : edges[2]].reshape(2, size),
    )


def solution(mesh):
    rows = P("shard", ("ctx", "tp"), None)
    flat = P(("shard", "ctx"), "tp")
    deep = P(("shard", "ctx"), None, "tp")
    return jax.shard_map(
        body,
        mesh=mesh,
        in_specs=(rows, rows, P("shard"), deep, flat, P(), flat, flat, deep, flat, P(), P(), P()),
        out_specs=(rows, rows, deep, flat, P(), flat, flat, deep, flat, P(), P(), P()),
        check_vma=False,
    )
```

```python
import functools
import math

import jax
import jax.numpy as jnp
from jax import lax
from jax.experimental import pallas as pl
from jax.experimental.pallas import tpu as pltpu
from jax.sharding import PartitionSpec as P

epsilon = 1e-06
f32 = jnp.float32
bf16 = jnp.bfloat16
BIG = 1e30
VMEM_LIMIT = 60 * 1024 * 1024


def mm(left, right):
    return jnp.dot(left, right, preferred_element_type=f32)


def mm_nt(left, right):
    return lax.dot_general(left, right, (((1,), (1,)), ((), ())), preferred_element_type=f32)


def mm_tn(left, right):
    return lax.dot_general(left, right, (((0,), (0,)), ((), ())), preferred_element_type=f32)


def whole(shape):
    return pl.BlockSpec(shape, lambda *_: (0,) * len(shape))


def call(kernel, outs, *operands, grid=None, in_specs=None, out_specs=None, scratch=(), blocks=None, places=None,
         weight=0.1):
    extra = {}
    if grid is None and blocks:
        grid = (1,)
        places = places or {}
        in_specs = [
            pl.BlockSpec(blocks.get(i, o.shape), functools.partial(lambda at, *_: at, places.get(i, (0,) * o.ndim)))
            for i, o in enumerate(operands)
        ]
        out_specs = [whole(o.shape) for o in outs]
    if grid is not None:
        extra = dict(grid=grid, in_specs=in_specs, out_specs=out_specs)
    return pl.pallas_call(
        kernel,
        out_shape=outs,
        scratch_shapes=list(scratch),
        compiler_params=pltpu.CompilerParams(vmem_limit_bytes=VMEM_LIMIT),
        cost_estimate=pl.CostEstimate(flops=int(weight * 1e9), bytes_accessed=int(weight * 1e6), transcendentals=0),
        **extra,
    )(*operands)


def sds(shape, dtype):
    return jax.ShapeDtypeStruct(shape, dtype)


def swap(value, axis, bit):
    n = lax.axis_size(axis)
    return lax.ppermute(value, axis, [(j, j ^ bit) for j in range(n)])


def gather_rows(own):
    n = lax.axis_size("tp")
    if n != 4:
        return [own] + [swap(own, "tp", k) for k in range(1, n)]
    far = swap(own, "tp", 2)
    near = swap(own, "tp", 1)
    return [own, near, far, swap(far, "tp", 1)]


def gather_all(own):
    n = lax.axis_size("tp")
    return lax.all_to_all(jnp.broadcast_to(own[None], (n,) + own.shape), "tp", 0, 0, tiled=True)


def scatter_all(blocks):
    return lax.all_to_all(blocks, "tp", 0, 0, tiled=True)


def send_rows(parts):
    n = lax.axis_size("tp")
    if n != 4:
        return [parts[0]] + [swap(parts[k], "tp", k) for k in range(1, n)]
    across = swap(parts[3], "tp", 1)
    near = swap(parts[1], "tp", 1)
    far = (parts[2].astype(f32) + across.astype(f32)).astype(bf16)
    return [parts[0], near, swap(far, "tp", 2)]


def after(value, *others):
    return lax.optimization_barrier((value, others))[0]


def pick(value, index, axis=0):
    return lax.dynamic_index_in_dim(value, index, axis, keepdims=False)


def scatter_weight(part):
    shards, halves = lax.axis_size("shard"), lax.axis_size("ctx")
    me, half = lax.axis_index("shard"), lax.axis_index("ctx")
    width, cols = part.shape
    blocks = part.reshape(shards, halves, width // (shards * halves), cols)
    got = swap(pick(blocks, 1 - half, 1), "ctx", 1)
    keep = pick(blocks, half, 1)

    def pair(k):
        return pick(keep, me ^ k).astype(f32) + pick(got, me ^ k).astype(f32)

    arrived = [swap(pair(k).astype(bf16), "shard", k) for k in range(1, shards)]
    return pair(0), arrived


def sum_over(value, axes):
    for axis in axes:
        n = lax.axis_size(axis)
        total = value
        for k in range(1, n):
            total = total + swap(value, axis, k)
        value = total
    return value


def thirds(value):
    high = value.astype(bf16)
    rest = value - high.astype(f32)
    middle = rest.astype(bf16)
    return high, middle, (rest - middle.astype(f32)).astype(bf16)


def head_sums(value, size):
    cols = value.shape[1]
    shape = (cols, cols)
    row = lax.broadcasted_iota(jnp.int32, shape, 0) // size
    col = lax.broadcasted_iota(jnp.int32, shape, 1) // size
    same = (row == col).astype(bf16)
    high = value.astype(bf16)
    low = (value - high.astype(f32)).astype(bf16)
    return mm(high, same) + mm(low, same)


def spread(pieces, rows):
    used = sum(p.shape[1] for p in pieces)
    return jnp.concatenate(list(pieces) + [jnp.zeros((rows, 128 - used), bf16)], axis=1)


def running(mask, value, heads):
    rows = value.shape[0]
    parts = thirds(value[:, :heads])
    total = mm(mask, spread(parts, rows))
    return total[:, :heads] + total[:, heads : 2 * heads] + total[:, 2 * heads : 3 * heads]


def project_kernel(heads, size, chunks, *refs):
    x_refs, refs = refs[:chunks], refs[chunks:]
    w_ref, gain_ref, qk_ref, bias_ref, rank_ref, rank_t_ref = refs[:6]
    (normed_ref, qa_ref, ka_ref, va_ref, send_ref, qraw_ref, kraw_ref, open_ref, pre_ref, cum_ref) = refs[6:]
    rows = x_refs[0].shape[0]
    span = rows * chunks
    cols = heads * size
    gain = gain_ref[...]
    for c in range(chunks):
        x = x_refs[c][...].astype(f32)
        r = lax.rsqrt(jnp.mean(x * x, axis=1, keepdims=True) + epsilon)
        normed_ref[c * rows : (c + 1) * rows, :] = (x * r * gain).astype(bf16)
    normed = normed_ref[...]
    pre = mm(normed, w_ref[:, 4 * cols : 4 * cols + 128]) + bias_ref[...]
    pre_ref[...] = pre
    logs = jnp.minimum(pre, 0.0) - jnp.log(1.0 + jnp.exp(-jnp.abs(pre)))
    earlier = (rank_t_ref[...] <= rank_ref[...]).astype(bf16)
    cum = running(earlier, logs, heads)
    cum_ref[...] = jnp.concatenate([cum, jnp.zeros((span, 128 - heads), f32)], axis=1)
    ones = jnp.ones((span, 3), bf16)
    fill = jnp.zeros((span, 128 - size - 6), bf16)
    cums = thirds(cum)
    outs = thirds(-cum)
    fars = thirds(jnp.sum(logs[:, :heads], axis=0, keepdims=True) - cum)

    def at(parts, h):
        return [p[:, h : h + 1] for p in parts]

    for which, raw_ref in ((0, qraw_ref), (1, kraw_ref)):
        raw = mm(normed, w_ref[:, (which + 1) * cols : (which + 2) * cols])
        raw_ref[...] = raw
        r = lax.rsqrt(head_sums(raw * raw, size) * (1.0 / size) + epsilon)
        value = (raw * r * qk_ref[which : which + 1, :]).astype(bf16)
        if which == 0:
            value = value * jnp.asarray(1.0 / math.sqrt(size), bf16)
            for h in range(heads):
                piece = value[:, h * size : (h + 1) * size]
                qa_ref[:, h * 128 : (h + 1) * 128] = jnp.concatenate([piece] + at(cums, h) + [ones, fill], axis=1)
        else:
            send_ref[:, 0:cols] = value
            for h in range(heads):
                piece = value[:, h * size : (h + 1) * size]
                ka_ref[:, h * 128 : (h + 1) * 128] = jnp.concatenate([piece, ones] + at(outs, h) + [fill], axis=1)
    value = mm(normed, w_ref[:, 3 * cols : 4 * cols]).astype(bf16)
    send_ref[:, cols : 2 * cols] = value
    tail = jnp.concatenate([ones, jnp.zeros((span, 128 - size - 3), bf16)], axis=1)
    for h in range(heads):
        va_ref[:, h * 128 : (h + 1) * 128] = jnp.concatenate([value[:, h * size : (h + 1) * size], tail], axis=1)
    send_ref[:, 2 * cols :] = spread(fars, span)
    open_ref[...] = jax.nn.sigmoid(mm(normed, w_ref[:, 4 * cols + 128 :]))


def attend_kernel(heads, size, qa_ref, ka_ref, va_ref, left_ref, open_ref, rank_ref, rank_t_ref, wout_ref,
                  gated_ref, att_ref, lse_ref, kl_ref, vl_ref, *branch_refs):
    cols = heads * size
    rows = qa_ref.shape[0]
    chunks = len(branch_refs)
    step = rows // chunks
    keep = rank_t_ref[...] <= rank_ref[...]
    shut = jnp.where(lax.axis_index("ctx") == 0, -BIG, 0.0).astype(bf16)
    ones = jnp.ones((rows, 3), bf16)
    fill = jnp.zeros((rows, 128 - size - 6), bf16)
    tail = jnp.zeros((rows, 128 - size - 3), bf16)
    lses = []
    for h in range(heads):
        wide = slice(h * 128, (h + 1) * 128)
        hs = slice(h * size, (h + 1) * size)
        far = [left_ref[:, 2 * cols + i * heads + h : 2 * cols + i * heads + h + 1] for i in range(3)]
        kl = jnp.concatenate([left_ref[:, hs], ones, far[0] + shut, far[1], far[2], fill], axis=1)
        vl = jnp.concatenate([left_ref[:, cols + h * size : cols + (h + 1) * size], ones, tail], axis=1)
        kl_ref[:, wide] = kl
        vl_ref[:, wide] = vl
        q = qa_ref[:, wide]
        el = jnp.exp(mm_nt(q, kl)).astype(bf16)
        er = jnp.exp(jnp.where(keep, mm_nt(q, ka_ref[:, wide]), -BIG)).astype(bf16)
        o = mm(el, vl) + mm(er, va_ref[:, wide])
        total = o[:, size : size + 1]
        att = o[:, :size] / total
        att_ref[:, hs] = att
        gated_ref[:, hs] = (att * open_ref[:, hs]).astype(bf16)
        lses.append(jnp.log(total))
    lse_ref[...] = jnp.concatenate(lses + [jnp.zeros((rows, 128 - heads), f32)], axis=1)
    branch = mm_nt(gated_ref[...], wout_ref[...]).astype(bf16)
    for c in range(chunks):
        branch_refs[c][...] = branch[c * step : (c + 1) * step, :]


def hidden_back_kernel(chunks, cot_ref, wd_ref, dh_ref, order_ref):
    me = lax.axis_index("tp")
    rows = cot_ref.shape[1]

    @pl.when(pl.program_id(0) == 0)
    def _():
        for c in range(chunks):
            order_ref[c * rows : (c + 1) * rows, :] = cot_ref[pl.ds(me ^ c, 1)][0]

    dh_ref[...] = mm(order_ref[...], wd_ref[...])


def ffn_kernel(steps, chunks, *refs):
    nm_refs, refs = refs[:chunks], refs[chunks:]
    dh_ref, wg_ref, wu_ref, nm_ref, hid_ref, dgu_ref = refs[:6]
    p_refs, refs = refs[6 : 6 + chunks], refs[6 + chunks :]
    w_all = refs[0]
    rows = nm_refs[0].shape[0]
    tile = wg_ref.shape[1]
    units = tile * steps
    j = pl.program_id(0)

    @pl.when(j == 0)
    def _():
        for c in range(chunks):
            nm_ref[c * rows : (c + 1) * rows, :] = nm_refs[c][...]

    gate = mm(nm_ref[...], wg_ref[...])
    up = mm(nm_ref[...], wu_ref[...])
    dh = dh_ref[...]
    sig = jax.nn.sigmoid(gate)
    act = gate * sig
    hid_ref[...] = (act * up).astype(bf16)
    dg = (dh * up * sig * (1.0 + gate * (1.0 - sig))).astype(bf16)
    du = (dh * act).astype(bf16)
    for s in range(steps):

        @pl.when(j == s)
        def _():
            at, up_at = slice(s * tile, (s + 1) * tile), slice(units + s * tile, units + (s + 1) * tile)
            dgu_ref[:, at] = dg
            dgu_ref[:, up_at] = du
            w_all[:, at] = wg_ref[...]
            w_all[:, up_at] = wu_ref[...]

    @pl.when(j == steps - 1)
    def _():
        width = w_all.shape[0]
        for b in range(0, width, 256):
            part = mm_nt(dgu_ref[...], w_all[b : b + 256, :]).astype(bf16)
            for c in range(chunks):
                p_refs[c][:, b : b + 256] = part[c * rows : (c + 1) * rows, :]


def down_kernel(chunks, hid_ref, wd_ref, out_ref):
    me = lax.axis_index("tp")
    down = mm_nt(hid_ref[...], wd_ref[...]).astype(bf16)
    rows = out_ref.shape[1]
    for c in range(chunks):
        out_ref[pl.ds(me ^ c, 1)] = down[c * rows : (c + 1) * rows, :][None]


def attend_back_kernel(heads, size, chunks, *refs):
    db_refs, refs = refs[:chunks], refs[chunks:]
    (qa_ref, ka_ref, va_ref, kl_ref, vl_ref, cum_ref, lse_ref, open_ref, att_ref, rank_ref, rank_t_ref,
     wout_ref) = refs[:12]
    branch_ref, dq_ref, dk_ref, dv_ref, back_ref, dopen_ref, dcum_ref = refs[12:]
    cols = heads * size
    part = db_refs[0].shape[0]
    rows = part * chunks
    for c in range(chunks):
        branch_ref[c * part : (c + 1) * part, :] = db_refs[c][...]
    keep = rank_t_ref[...] >= rank_ref[...]
    dg = mm(branch_ref[...], wout_ref[...])
    op = open_ref[...]
    att = att_ref[...]
    dopen_ref[...] = (dg * att * op * (1.0 - op)).astype(bf16)
    da_all = (dg * op).astype(bf16)
    prod = da_all.astype(f32) * att
    place = thirds(cum_ref[:, :heads] - lse_ref[:, :heads])
    ones = jnp.ones((rows, 3), bf16)
    fill = jnp.zeros((rows, 128 - size - 6), bf16)
    tail = jnp.zeros((rows, 128 - size - 3), bf16)
    owns, lefts = [], []
    for h in range(heads):
        wide = slice(h * 128, (h + 1) * 128)
        hs = slice(h * size, (h + 1) * size)
        vs = slice(cols + h * size, cols + (h + 1) * size)
        q = jnp.concatenate([qa_ref[:, h * 128 : h * 128 + size]] + [p[:, h : h + 1] for p in place] + [ones, fill], axis=1)
        delta = thirds(-jnp.sum(prod[:, hs], axis=1, keepdims=True))
        da = jnp.concatenate([da_all[:, hs], delta[0], delta[1], delta[2], tail], axis=1)
        dq = jnp.zeros((rows, 128), f32)
        found = []
        for k_ref, v_ref, right in ((kl_ref, vl_ref, False), (ka_ref, va_ref, True)):
            k, v = k_ref[:, wide], v_ref[:, wide]
            score = mm_nt(k, q)
            if right:
                score = jnp.where(keep, score, -BIG)
            p = jnp.exp(score)
            ds = (p * mm_nt(v, da)).astype(bf16)
            found += [mm(p.astype(bf16), da)[:, :size], mm(ds, q)]
            dq = dq + mm_tn(ds, k)
        dq_ref[:, hs] = dq[:, :size] * (1.0 / math.sqrt(size))
        back_ref[:, vs] = found[0].astype(bf16)
        back_ref[:, hs] = found[1][:, :size].astype(bf16)
        dv_ref[:, hs] = found[2]
        dk_ref[:, hs] = found[3][:, :size]
        lefts.append(-found[1][:, size + 3 : size + 4])
        owns.append(dq[:, size : size + 1] - found[3][:, size + 3 : size + 4])
    own = jnp.concatenate(owns, axis=1)
    dcum_ref[...] = jnp.concatenate([own, jnp.zeros((rows, 128 - heads), f32)], axis=1)
    total = jnp.broadcast_to(jnp.sum(own, axis=0, keepdims=True), (rows, heads))
    sent = thirds(jnp.concatenate(lefts, axis=1)) + thirds(total)
    back_ref[:, 2 * cols :] = spread(sent, rows)


def project_back_kernel(heads, size, chunks, *refs):
    x_refs, refs = refs[:chunks], refs[chunks:]
    (w_ref, qk_ref, qraw_ref, kraw_ref, dq_ref, dk_ref, dv_ref, back_ref, dopen_ref, dcum_ref, pre_ref, rank_ref,
     rank_t_ref, gm_ref) = refs[:14]
    mixed_ref, out_ref = refs[14:]
    cols = heads * size
    width = x_refs[0].shape[1]
    rows = x_refs[0].shape[0]
    span = rows * chunks
    sums = []
    for which, raw_ref in ((0, qraw_ref), (1, kraw_ref)):
        d = dq_ref[...] if which == 0 else dk_ref[...] + back_ref[:, :cols].astype(f32)
        raw = raw_ref[...]
        r = lax.rsqrt(head_sums(raw * raw, size) * (1.0 / size) + epsilon)
        u = raw * r
        total = jnp.sum(d * u, axis=0, keepdims=True)
        sums.append(sum(total[:, h * size : (h + 1) * size] for h in range(heads)))
        e = d * qk_ref[which : which + 1, :]
        mixed_ref[:, which * cols : (which + 1) * cols] = (
            r * (e - u * (head_sums(e * u, size) * (1.0 / size)))
        ).astype(bf16)
    mixed_ref[:, 2 * cols : 3 * cols] = (dv_ref[...] + back_ref[:, cols : 2 * cols].astype(f32)).astype(bf16)
    mixed_ref[:, 3 * cols + 128 :] = dopen_ref[...]
    extra = back_ref[:, 2 * cols :].astype(f32)
    got = extra[:, :heads] + extra[:, heads : 2 * heads] + extra[:, 2 * heads : 3 * heads]
    after_sum = extra[:, 3 * heads : 4 * heads] + extra[:, 4 * heads : 5 * heads] + extra[:, 5 * heads : 6 * heads]
    later = (rank_t_ref[...] >= rank_ref[...]).astype(bf16)
    dlog = running(later, dcum_ref[:, :heads] + got, heads) + after_sum
    df = jnp.concatenate([dlog, jnp.zeros((span, 128 - heads), f32)], axis=1) * jax.nn.sigmoid(-pre_ref[...])
    bias = jnp.sum(df, axis=0, keepdims=True)
    mixed_ref[:, 3 * cols : 3 * cols + 128] = df.astype(bf16)
    me = lax.axis_index("tp")
    units = []
    for c in range(chunks):
        x = x_refs[c][...].astype(f32)
        units.append(x * lax.rsqrt(jnp.mean(x * x, axis=1, keepdims=True) + epsilon))
    gains = []
    for b in range(0, width, 256):
        dn = mm_nt(mixed_ref[...], w_ref[b : b + 256, cols:])
        gain = jnp.zeros((1, 256), f32)
        for c in range(chunks):
            piece = dn[c * rows : (c + 1) * rows, :]
            out_ref[pl.ds(me ^ c, 1), 0:rows, b : b + 256] = piece.astype(bf16)[None]
            gain = gain + jnp.sum(piece * units[c][:, b : b + 256], axis=0, keepdims=True)
        gains.append(gain)
    gain = jnp.concatenate(gains, axis=1)
    bias = pltpu.roll(bias, me * heads, 1)
    lanes = jnp.concatenate([sums[0], sums[1], bias, jnp.zeros((1, width - 2 * size - 128), f32)], axis=1)
    low = jnp.concatenate([gain, lanes, gm_ref[...], jnp.zeros((13, width), f32)], axis=0).astype(bf16)
    for c in range(chunks):
        out_ref[c, rows : rows + 16, :] = low


def middle_kernel(x_ref, gain_ref, *refs):
    middle = x_ref[...].astype(f32)
    for ref in refs[:-2]:
        middle = middle + ref[...].astype(f32)
    mid_ref, nm_ref = refs[-2:]
    mid_ref[...] = middle
    r = lax.rsqrt(jnp.mean(middle * middle, axis=1, keepdims=True) + epsilon)
    nm_ref[...] = (middle * r * gain_ref[...]).astype(bf16)


def norm_back(d, v, gain):
    r = lax.rsqrt(jnp.mean(v * v, axis=1, keepdims=True) + epsilon)
    u = v * r
    e = d * gain
    return r * (e - u * jnp.mean(e * u, axis=1, keepdims=True)), jnp.sum(d * u, axis=0, keepdims=True)


def middle_back_kernel(mid_ref, cot_ref, gain_ref, *refs):
    d = refs[0][...].astype(f32)
    for ref in refs[1:-3]:
        d = d + ref[...].astype(f32)
    dmid_ref, branch_ref, part_ref = refs[-3:]
    back, part = norm_back(d, mid_ref[...], gain_ref[...])
    back = back + cot_ref[...].astype(f32)
    dmid_ref[...] = back
    branch_ref[...] = back.astype(bf16)
    part_ref[...] = part


def input_back_kernel(x_ref, dmid_ref, gain_ref, *refs):
    rows = x_ref.shape[0]
    out_ref = refs[-1]
    d = refs[0][0, 0:rows, :].astype(f32)
    for c in range(1, refs[0].shape[0]):
        d = d + refs[0][c, 0:rows, :].astype(f32)
    back, _ = norm_back(d, x_ref[...].astype(f32), gain_ref[...])
    out_ref[...] = (back + dmid_ref[...]).astype(bf16)


def finish_ffn_kernel(in_ref, gu_ref, down_ref):
    units = down_ref.shape[1]
    gu_ref[:, 0, :] = in_ref[:, :units].astype(f32)
    gu_ref[:, 1, :] = in_ref[:, units : 2 * units].astype(f32)
    down_ref[...] = in_ref[:, 2 * units :].astype(f32)


def finish_gates_kernel(in_ref, out_ref, gate_ref):
    cols = out_ref.shape[1]
    out_ref[...] = in_ref[:, :cols].astype(f32)
    gate_ref[...] = in_ref[:, cols:].astype(f32)


def finish_qkv_kernel(own_ref, *refs):
    qkv_ref, forget_ref = refs[-2:]
    cols = qkv_ref.shape[2]
    total = own_ref[...]
    for ref in refs[:-2]:
        total = total + ref[...].astype(f32)
    for i in range(3):
        qkv_ref[:, i, :] = total[:, i * cols : (i + 1) * cols]
    forget_ref[...] = total[:, 3 * cols : 3 * cols + forget_ref.shape[1]]


def body(tokens, cotangent, lengths, w_qkv, w_forget, forget_bias, w_ogate, w_out, w_gu, w_down, gain_attn, gain_mlp,
         qk_gain):
    slots, rows, width = tokens.shape
    assert slots == 1
    n = lax.axis_size("tp")
    me = lax.axis_index("tp")
    half = lax.axis_index("ctx")
    both = ("shard", "ctx")
    span = rows * n
    heads = w_forget.shape[1]
    size = qk_gain.shape[1]
    cols = heads * size
    units = w_down.shape[1]
    slab = w_qkv.shape[0]

    x_own = tokens[0]
    x_parts = gather_rows(x_own)

    own_pos = half * span + me * rows + jnp.arange(rows, dtype=jnp.int32)
    valid = (own_pos < lengths[0]).astype(f32)[:, None]
    cot_own = (cotangent[0].astype(f32) * valid).astype(bf16)
    cot = gather_all(after(cot_own, *x_parts))

    order = jnp.concatenate([(me ^ k) * rows + jnp.arange(rows, dtype=jnp.int32) for k in range(n)])
    rank, rank_t = order[:, None], order[None, :]

    first = jnp.concatenate(
        [w_out, w_qkv.reshape(slab, 3 * cols), w_forget, jnp.zeros((slab, 128 - heads), bf16), w_ogate], axis=1
    )
    first = lax.all_gather(first, both, axis=0, tiled=True)
    rest = jnp.concatenate([w_gu.reshape(slab, 2 * units), w_down], axis=1)
    rest = lax.all_gather(rest, both, axis=0, tiled=True)
    wide = 4 * cols + 128
    w_out_full, out_block = first, (width, cols)
    if cols % 128:
        w_out_full = first[:, :cols]

    bias = lax.dynamic_slice_in_dim(forget_bias, me * heads, heads)
    bias = jnp.concatenate([bias, jnp.zeros((128 - heads,), f32)])[None, :]
    gain_a, gain_m = gain_attn[None, :], gain_mlp[None, :]
    qk_wide = jnp.tile(qk_gain, (1, heads))

    normed, qa, ka, va, sent, qraw, kraw, opener, pre, cum = call(
        functools.partial(project_kernel, heads, size, n),
        [
            sds((span, width), bf16),
            sds((span, heads * 128), bf16),
            sds((span, heads * 128), bf16),
            sds((span, heads * 128), bf16),
            sds((span, 2 * cols + 128), bf16),
            sds((span, cols), f32),
            sds((span, cols), f32),
            sds((span, cols), f32),
            sds((span, 128), f32),
            sds((span, 128), f32),
        ],
        *x_parts, first, gain_a, qk_wide, bias, rank, rank_t,
    )
    left = lax.ppermute(sent, "ctx", [(0, 1)])
    gated, attended, lse, kl, vl, *branch = call(
        functools.partial(attend_kernel, heads, size),
        [sds((span, cols), bf16), sds((span, cols), f32), sds((span, 128), f32)]
        + [sds((span, heads * 128), bf16)] * 2
        + [sds((rows, width), bf16)] * n,
        qa, ka, va, left, opener, rank, rank_t, w_out_full,
        blocks={7: out_block},
    )
    middle, nm_own = call(
        middle_kernel,
        [sds((rows, width), f32), sds((rows, width), bf16)],
        x_own, gain_m, *send_rows(after(branch, cot)),
    )
    tile = min(512, units)
    steps = units // tile
    d_hidden, cot = call(
        functools.partial(hidden_back_kernel, n),
        [sds((span, units), f32), sds((span, width), bf16)],
        after(cot, nm_own), rest,
        grid=(steps,),
        in_specs=[whole((n, rows, width)), pl.BlockSpec((width, tile), lambda j: (0, j + 2 * steps))],
        out_specs=[pl.BlockSpec((span, tile), lambda j: (0, j)), whole((span, width))],
    )
    nm_parts = after(gather_rows(nm_own), d_hidden)
    nm, hidden, d_units, *p_parts = call(
        functools.partial(ffn_kernel, steps, n),
        [sds((span, width), bf16), sds((span, units), bf16), sds((span, 2 * units), bf16)]
        + [sds((rows, width), bf16)] * n,
        *nm_parts, d_hidden, rest, rest,
        grid=(steps,),
        in_specs=[whole((rows, width))] * n
        + [
            pl.BlockSpec((span, tile), lambda j: (0, j)),
            pl.BlockSpec((width, tile), lambda j: (0, j)),
            pl.BlockSpec((width, tile), lambda j: (0, j + steps)),
        ],
        out_specs=[whole((span, width)), pl.BlockSpec((span, tile), lambda j: (0, j)), whole((span, 2 * units))]
        + [whole((rows, width))] * n,
        scratch=[pltpu.VMEM((width, 2 * units), bf16)],
    )
    p_got = send_rows(p_parts)
    part_ffn = jnp.concatenate([mm_tn(nm, d_units).astype(bf16), mm_tn(cot, hidden).astype(bf16)], axis=1)
    grad_ffn = lax.psum_scatter(after(part_ffn, p_got[1]), both, scatter_dimension=0, tiled=True)
    d_middle, db_own, gain_m_part = call(
        middle_back_kernel,
        [sds((rows, width), f32), sds((rows, width), bf16), sds((1, width), f32)],
        middle, cot_own, gain_m, *after(p_got, part_ffn),
    )
    db_parts = gather_rows(db_own)
    (down_rows,) = call(
        functools.partial(down_kernel, n),
        [sds((n, rows, width), bf16)],
        after(hidden, db_own), rest,
        blocks={1: (width, units)}, places={1: (0, 2)},
    )
    down = scatter_all(after(down_rows, db_parts))
    d_branch, dq, dk, dv, back, d_open, d_cum = call(
        functools.partial(attend_back_kernel, heads, size, n),
        [
            sds((span, width), bf16),
            sds((span, cols), f32),
            sds((span, cols), f32),
            sds((span, cols), f32),
            sds((span, 2 * cols + 128), bf16),
            sds((span, cols), bf16),
            sds((span, 128), f32),
        ],
        *after(db_parts, down_rows), qa, ka, va, kl, vl, cum, lse, opener, attended, rank, rank_t, w_out_full,
        blocks={n + 11: out_block}, weight=100,
    )
    part_gates = jnp.concatenate([mm_tn(d_branch, gated), mm_tn(normed, d_open)], axis=1).astype(bf16)
    back = lax.ppermute(back, "ctx", [(1, 0)])
    mixed, dn = call(
        functools.partial(project_back_kernel, heads, size, n),
        [sds((span, wide), bf16), sds((n, rows + 16, width), bf16)],
        *x_parts, first, qk_wide, qraw, kraw, dq, dk, dv, back, d_open, d_cum, pre, rank, rank_t, gain_m_part,
    )
    down_sum = jnp.sum(after(down, mixed).astype(f32), axis=0)
    output = (valid * (middle + down_sum)).astype(bf16)
    deep = 3 * cols + 128
    grad_gates = lax.psum_scatter(after(part_gates, mixed, grad_ffn), both, scatter_dimension=0, tiled=True)
    state_qkv = scatter_weight(mm_tn(normed, mixed[:, :deep]).astype(bf16))
    dn = scatter_all(after(dn, output, grad_ffn))
    grad_gu, grad_down = call(
        finish_ffn_kernel, [sds((slab, 2, units), f32), sds((slab, units), f32)], grad_ffn
    )
    dn_late, grad_gu, grad_down, _ = lax.optimization_barrier((dn, grad_gu, grad_down, state_qkv[1]))
    (input_grad,) = call(
        input_back_kernel, [sds((rows, width), bf16)], x_own, d_middle, gain_a, dn_late
    )
    grad_out, grad_ogate = call(finish_gates_kernel, [sds((slab, cols), f32)] * 2, grad_gates)
    grad_qkv, grad_forget = call(
        finish_qkv_kernel,
        [sds((slab, 3, cols), f32), sds((slab, heads), f32)],
        state_qkv[0], *state_qkv[1],
    )

    sums = jnp.sum(dn[:, rows:].astype(f32), axis=0)
    small = jnp.concatenate([sums[0], sums[1, : 2 * size + n * heads], sums[2]])
    small = sum_over(small, ("ctx", "shard"))
    edges = [0, width, width + 2 * size, width + 2 * size + n * heads]
    return (
        output[None],
        input_grad[None],
        grad_qkv,
        grad_forget,
        small[edges[2] : edges[3]],
        grad_ogate,
        grad_out,
        grad_gu,
        grad_down,
        small[edges[0] : edges[1]],
        small[edges[2] + n * heads :],
        small[edges[1] : edges[2]].reshape(2, size),
    )


def solution(mesh):
    rows = P("shard", ("ctx", "tp"), None)
    flat = P(("shard", "ctx"), "tp")
    deep = P(("shard", "ctx"), None, "tp")
    return jax.shard_map(
        body,
        mesh=mesh,
        in_specs=(rows, rows, P("shard"), deep, flat, P(), flat, flat, deep, flat, P(), P(), P()),
        out_specs=(rows, rows, deep, flat, P(), flat, flat, deep, flat, P(), P(), P()),
        check_vma=False,
    )
```

```python
import functools
import math

import jax
import jax.numpy as jnp
from jax import lax
from jax.experimental import pallas as pl
from jax.experimental.pallas import tpu as pltpu
from jax.sharding import PartitionSpec as P

epsilon = 1e-06
f32 = jnp.float32
bf16 = jnp.bfloat16
BIG = 1e30
VMEM_LIMIT = 60 * 1024 * 1024


def mm(left, right):
    return jnp.dot(left, right, preferred_element_type=f32)


def mm_nt(left, right):
    return lax.dot_general(left, right, (((1,), (1,)), ((), ())), preferred_element_type=f32)


def mm_tn(left, right):
    return lax.dot_general(left, right, (((0,), (0,)), ((), ())), preferred_element_type=f32)


def whole(shape):
    return pl.BlockSpec(shape, lambda *_: (0,) * len(shape))


def call(kernel, outs, *operands, grid=None, in_specs=None, out_specs=None, scratch=(), blocks=None, places=None,
         weight=0.1):
    extra = {}
    if grid is None and blocks:
        grid = (1,)
        places = places or {}
        in_specs = [
            pl.BlockSpec(blocks.get(i, o.shape), functools.partial(lambda at, *_: at, places.get(i, (0,) * o.ndim)))
            for i, o in enumerate(operands)
        ]
        out_specs = [whole(o.shape) for o in outs]
    if grid is not None:
        extra = dict(grid=grid, in_specs=in_specs, out_specs=out_specs)
    return pl.pallas_call(
        kernel,
        out_shape=outs,
        scratch_shapes=list(scratch),
        compiler_params=pltpu.CompilerParams(vmem_limit_bytes=VMEM_LIMIT),
        cost_estimate=pl.CostEstimate(flops=int(weight * 1e9), bytes_accessed=int(weight * 1e6), transcendentals=0),
        **extra,
    )(*operands)


def sds(shape, dtype):
    return jax.ShapeDtypeStruct(shape, dtype)


def swap(value, axis, bit):
    n = lax.axis_size(axis)
    return lax.ppermute(value, axis, [(j, j ^ bit) for j in range(n)])


def gather_rows(own):
    n = lax.axis_size("tp")
    if n != 4:
        return [own] + [swap(own, "tp", k) for k in range(1, n)]
    far = swap(own, "tp", 2)
    near = swap(own, "tp", 1)
    return [own, near, far, swap(far, "tp", 1)]


def gather_all(own):
    n = lax.axis_size("tp")
    return lax.all_to_all(jnp.broadcast_to(own[None], (n,) + own.shape), "tp", 0, 0, tiled=True)


def scatter_all(blocks):
    return lax.all_to_all(blocks, "tp", 0, 0, tiled=True)


def send_rows(parts, *late):
    n = lax.axis_size("tp")
    if n != 4:
        return [parts[0]] + [swap(parts[k], "tp", k) for k in range(1, n)]
    across = swap(parts[3], "tp", 1)
    near = swap(after(parts[1], *late) if late else parts[1], "tp", 1)
    far = (parts[2].astype(f32) + across.astype(f32)).astype(bf16)
    return [parts[0], near, swap(far, "tp", 2)]


def after(value, *others):
    return lax.optimization_barrier((value, others))[0]


def sum_over(value, axes):
    for axis in axes:
        n = lax.axis_size(axis)
        total = value
        for k in range(1, n):
            total = total + swap(value, axis, k)
        value = total
    return value


def thirds(value):
    high = value.astype(bf16)
    rest = value - high.astype(f32)
    middle = rest.astype(bf16)
    return high, middle, (rest - middle.astype(f32)).astype(bf16)


def head_sums(value, size):
    cols = value.shape[1]
    shape = (cols, cols)
    row = lax.broadcasted_iota(jnp.int32, shape, 0) // size
    col = lax.broadcasted_iota(jnp.int32, shape, 1) // size
    same = (row == col).astype(bf16)
    high = value.astype(bf16)
    low = (value - high.astype(f32)).astype(bf16)
    return mm(high, same) + mm(low, same)


def spread(pieces, rows):
    used = sum(p.shape[1] for p in pieces)
    return jnp.concatenate(list(pieces) + [jnp.zeros((rows, 128 - used), bf16)], axis=1)


def running(mask, value, heads):
    rows = value.shape[0]
    parts = thirds(value[:, :heads])
    total = mm(mask, spread(parts, rows))
    return total[:, :heads] + total[:, heads : 2 * heads] + total[:, 2 * heads : 3 * heads]


def project_kernel(heads, size, chunks, *refs):
    x_refs, refs = refs[:chunks], refs[chunks:]
    w_ref, gain_ref, qk_ref, bias_ref, rank_ref, rank_t_ref = refs[:6]
    (normed_ref, qa_ref, ka_ref, va_ref, send_ref, qraw_ref, kraw_ref, open_ref, pre_ref, cum_ref) = refs[6:]
    rows = x_refs[0].shape[0]
    span = rows * chunks
    cols = heads * size
    gain = gain_ref[...]
    for c in range(chunks):
        x = x_refs[c][...].astype(f32)
        r = lax.rsqrt(jnp.mean(x * x, axis=1, keepdims=True) + epsilon)
        normed_ref[c * rows : (c + 1) * rows, :] = (x * r * gain).astype(bf16)
    normed = normed_ref[...]
    pre = mm(normed, w_ref[:, 4 * cols : 4 * cols + 128]) + bias_ref[...]
    pre_ref[...] = pre
    logs = jnp.minimum(pre, 0.0) - jnp.log(1.0 + jnp.exp(-jnp.abs(pre)))
    earlier = (rank_t_ref[...] <= rank_ref[...]).astype(bf16)
    cum = running(earlier, logs, heads)
    cum_ref[...] = jnp.concatenate([cum, jnp.zeros((span, 128 - heads), f32)], axis=1)
    ones = jnp.ones((span, 3), bf16)
    fill = jnp.zeros((span, 128 - size - 6), bf16)
    cums = thirds(cum)
    outs = thirds(-cum)
    fars = thirds(jnp.sum(logs[:, :heads], axis=0, keepdims=True) - cum)

    def at(parts, h):
        return [p[:, h : h + 1] for p in parts]

    for which, raw_ref in ((0, qraw_ref), (1, kraw_ref)):
        raw = mm(normed, w_ref[:, (which + 1) * cols : (which + 2) * cols])
        raw_ref[...] = raw
        r = lax.rsqrt(head_sums(raw * raw, size) * (1.0 / size) + epsilon)
        value = (raw * r * qk_ref[which : which + 1, :]).astype(bf16)
        if which == 0:
            value = value * jnp.asarray(1.0 / math.sqrt(size), bf16)
            for h in range(heads):
                piece = value[:, h * size : (h + 1) * size]
                qa_ref[:, h * 128 : (h + 1) * 128] = jnp.concatenate([piece] + at(cums, h) + [ones, fill], axis=1)
        else:
            send_ref[:, 0:cols] = value
            for h in range(heads):
                piece = value[:, h * size : (h + 1) * size]
                ka_ref[:, h * 128 : (h + 1) * 128] = jnp.concatenate([piece, ones] + at(outs, h) + [fill], axis=1)
    value = mm(normed, w_ref[:, 3 * cols : 4 * cols]).astype(bf16)
    send_ref[:, cols : 2 * cols] = value
    tail = jnp.concatenate([ones, jnp.zeros((span, 128 - size - 3), bf16)], axis=1)
    for h in range(heads):
        va_ref[:, h * 128 : (h + 1) * 128] = jnp.concatenate([value[:, h * size : (h + 1) * size], tail], axis=1)
    send_ref[:, 2 * cols :] = spread(fars, span)
    open_ref[...] = jax.nn.sigmoid(mm(normed, w_ref[:, 4 * cols + 128 :]))


def attend_kernel(heads, size, qa_ref, ka_ref, va_ref, left_ref, open_ref, rank_ref, rank_t_ref, wout_ref,
                  gated_ref, att_ref, lse_ref, kl_ref, vl_ref, *branch_refs):
    cols = heads * size
    rows = qa_ref.shape[0]
    chunks = len(branch_refs)
    step = rows // chunks
    keep = rank_t_ref[...] <= rank_ref[...]
    shut = jnp.where(lax.axis_index("ctx") == 0, -BIG, 0.0).astype(bf16)
    ones = jnp.ones((rows, 3), bf16)
    fill = jnp.zeros((rows, 128 - size - 6), bf16)
    tail = jnp.zeros((rows, 128 - size - 3), bf16)
    lses = []
    for h in range(heads):
        wide = slice(h * 128, (h + 1) * 128)
        hs = slice(h * size, (h + 1) * size)
        far = [left_ref[:, 2 * cols + i * heads + h : 2 * cols + i * heads + h + 1] for i in range(3)]
        kl = jnp.concatenate([left_ref[:, hs], ones, far[0] + shut, far[1], far[2], fill], axis=1)
        vl = jnp.concatenate([left_ref[:, cols + h * size : cols + (h + 1) * size], ones, tail], axis=1)
        kl_ref[:, wide] = kl
        vl_ref[:, wide] = vl
        q = qa_ref[:, wide]
        el = jnp.exp(mm_nt(q, kl)).astype(bf16)
        er = jnp.exp(jnp.where(keep, mm_nt(q, ka_ref[:, wide]), -BIG)).astype(bf16)
        o = mm(el, vl) + mm(er, va_ref[:, wide])
        total = o[:, size : size + 1]
        att = o[:, :size] / total
        att_ref[:, hs] = att
        gated_ref[:, hs] = (att * open_ref[:, hs]).astype(bf16)
        lses.append(jnp.log(total))
    lse_ref[...] = jnp.concatenate(lses + [jnp.zeros((rows, 128 - heads), f32)], axis=1)
    branch = mm_nt(gated_ref[...], wout_ref[...]).astype(bf16)
    for c in range(chunks):
        branch_refs[c][...] = branch[c * step : (c + 1) * step, :]


def hidden_back_kernel(chunks, cot_ref, normed_ref, wd_ref, dh_ref, order_ref, flip_ref):
    me = lax.axis_index("tp")
    rows = cot_ref.shape[1]

    @pl.when(pl.program_id(0) == 0)
    def _():
        for c in range(chunks):
            order_ref[c * rows : (c + 1) * rows, :] = cot_ref[pl.ds(me ^ c, 1)][0]
        flip_ref[...] = jnp.transpose(normed_ref[...])

    dh_ref[...] = mm(order_ref[...], wd_ref[...])


def ffn_kernel(steps, chunks, *refs):
    nm_refs, refs = refs[:chunks], refs[chunks:]
    dh_ref, wg_ref, wu_ref, nm_ref, hid_ref, dgu_ref = refs[:6]
    p_refs, refs = refs[6 : 6 + chunks], refs[6 + chunks :]
    w_all = refs[0]
    rows = nm_refs[0].shape[0]
    tile = wg_ref.shape[1]
    units = tile * steps
    j = pl.program_id(0)

    @pl.when(j == 0)
    def _():
        for c in range(chunks):
            nm_ref[c * rows : (c + 1) * rows, :] = nm_refs[c][...]

    gate = mm(nm_ref[...], wg_ref[...])
    up = mm(nm_ref[...], wu_ref[...])
    dh = dh_ref[...]
    sig = jax.nn.sigmoid(gate)
    act = gate * sig
    hid_ref[...] = (act * up).astype(bf16)
    dg = (dh * up * sig * (1.0 + gate * (1.0 - sig))).astype(bf16)
    du = (dh * act).astype(bf16)
    for s in range(steps):

        @pl.when(j == s)
        def _():
            at, up_at = slice(s * tile, (s + 1) * tile), slice(units + s * tile, units + (s + 1) * tile)
            dgu_ref[:, at] = dg
            dgu_ref[:, up_at] = du
            w_all[:, at] = wg_ref[...]
            w_all[:, up_at] = wu_ref[...]

    @pl.when(j == steps - 1)
    def _():
        width = w_all.shape[0]
        for b in range(0, width, 256):
            part = mm_nt(dgu_ref[...], w_all[b : b + 256, :]).astype(bf16)
            for c in range(chunks):
                p_refs[c][:, b : b + 256] = part[c * rows : (c + 1) * rows, :]


def down_kernel(chunks, hid_ref, wd_ref, out_ref):
    me = lax.axis_index("tp")
    down = mm_nt(hid_ref[...], wd_ref[...]).astype(bf16)
    rows = out_ref.shape[1]
    for c in range(chunks):
        out_ref[pl.ds(me ^ c, 1)] = down[c * rows : (c + 1) * rows, :][None]


def attend_back_kernel(heads, size, chunks, *refs):
    db_refs, refs = refs[:chunks], refs[chunks:]
    (qa_ref, ka_ref, va_ref, kl_ref, vl_ref, cum_ref, lse_ref, open_ref, att_ref, rank_ref, rank_t_ref,
     wout_ref) = refs[:12]
    branch_ref, dq_ref, dk_ref, dv_ref, back_ref, dopen_ref, dcum_ref = refs[12:]
    cols = heads * size
    part = db_refs[0].shape[0]
    rows = part * chunks
    for c in range(chunks):
        branch_ref[c * part : (c + 1) * part, :] = db_refs[c][...]
    keep = rank_t_ref[...] >= rank_ref[...]
    dg = mm(branch_ref[...], wout_ref[...])
    op = open_ref[...]
    att = att_ref[...]
    dopen_ref[...] = (dg * att * op * (1.0 - op)).astype(bf16)
    da_all = (dg * op).astype(bf16)
    prod = da_all.astype(f32) * att
    place = thirds(cum_ref[:, :heads] - lse_ref[:, :heads])
    ones = jnp.ones((rows, 3), bf16)
    fill = jnp.zeros((rows, 128 - size - 6), bf16)
    tail = jnp.zeros((rows, 128 - size - 3), bf16)
    owns, lefts = [], []
    for h in range(heads):
        wide = slice(h * 128, (h + 1) * 128)
        hs = slice(h * size, (h + 1) * size)
        vs = slice(cols + h * size, cols + (h + 1) * size)
        q = jnp.concatenate([qa_ref[:, h * 128 : h * 128 + size]] + [p[:, h : h + 1] for p in place] + [ones, fill], axis=1)
        delta = thirds(-jnp.sum(prod[:, hs], axis=1, keepdims=True))
        da = jnp.concatenate([da_all[:, hs], delta[0], delta[1], delta[2], tail], axis=1)
        dq = jnp.zeros((rows, 128), f32)
        found = []
        for k_ref, v_ref, right in ((kl_ref, vl_ref, False), (ka_ref, va_ref, True)):
            k, v = k_ref[:, wide], v_ref[:, wide]
            score = mm_nt(k, q)
            if right:
                score = jnp.where(keep, score, -BIG)
            p = jnp.exp(score)
            ds = (p * mm_nt(v, da)).astype(bf16)
            found += [mm(p.astype(bf16), da)[:, :size], mm(ds, q)]
            dq = dq + mm_tn(ds, k)
        dq_ref[:, hs] = dq[:, :size] * (1.0 / math.sqrt(size))
        back_ref[:, vs] = found[0].astype(bf16)
        back_ref[:, hs] = found[1][:, :size].astype(bf16)
        dv_ref[:, hs] = found[2]
        dk_ref[:, hs] = found[3][:, :size]
        lefts.append(-found[1][:, size + 3 : size + 4])
        owns.append(dq[:, size : size + 1] - found[3][:, size + 3 : size + 4])
    own = jnp.concatenate(owns, axis=1)
    dcum_ref[...] = jnp.concatenate([own, jnp.zeros((rows, 128 - heads), f32)], axis=1)
    total = jnp.broadcast_to(jnp.sum(own, axis=0, keepdims=True), (rows, heads))
    sent = thirds(jnp.concatenate(lefts, axis=1)) + thirds(total)
    back_ref[:, 2 * cols :] = spread(sent, rows)


def project_back_kernel(heads, size, chunks, *refs):
    x_refs, refs = refs[:chunks], refs[chunks:]
    (w_ref, qk_ref, qraw_ref, kraw_ref, dq_ref, dk_ref, dv_ref, back_ref, dopen_ref, dcum_ref, pre_ref, rank_ref,
     rank_t_ref, gm_ref) = refs[:14]
    mixed_ref, out_refs = refs[14], refs[15:]
    cols = heads * size
    width = x_refs[0].shape[1]
    rows = x_refs[0].shape[0]
    span = rows * chunks
    sums = []
    for which, raw_ref in ((0, qraw_ref), (1, kraw_ref)):
        d = dq_ref[...] if which == 0 else dk_ref[...] + back_ref[:, :cols].astype(f32)
        raw = raw_ref[...]
        r = lax.rsqrt(head_sums(raw * raw, size) * (1.0 / size) + epsilon)
        u = raw * r
        total = jnp.sum(d * u, axis=0, keepdims=True)
        sums.append(sum(total[:, h * size : (h + 1) * size] for h in range(heads)))
        e = d * qk_ref[which : which + 1, :]
        mixed_ref[:, which * cols : (which + 1) * cols] = (
            r * (e - u * (head_sums(e * u, size) * (1.0 / size)))
        ).astype(bf16)
    mixed_ref[:, 2 * cols : 3 * cols] = (dv_ref[...] + back_ref[:, cols : 2 * cols].astype(f32)).astype(bf16)
    mixed_ref[:, 3 * cols + 128 :] = dopen_ref[...]
    extra = back_ref[:, 2 * cols :].astype(f32)
    got = extra[:, :heads] + extra[:, heads : 2 * heads] + extra[:, 2 * heads : 3 * heads]
    after_sum = extra[:, 3 * heads : 4 * heads] + extra[:, 4 * heads : 5 * heads] + extra[:, 5 * heads : 6 * heads]
    later = (rank_t_ref[...] >= rank_ref[...]).astype(bf16)
    dlog = running(later, dcum_ref[:, :heads] + got, heads) + after_sum
    df = jnp.concatenate([dlog, jnp.zeros((span, 128 - heads), f32)], axis=1) * jax.nn.sigmoid(-pre_ref[...])
    bias = jnp.sum(df, axis=0, keepdims=True)
    mixed_ref[:, 3 * cols : 3 * cols + 128] = df.astype(bf16)
    me = lax.axis_index("tp")
    units = []
    for c in range(chunks):
        x = x_refs[c][...].astype(f32)
        units.append(x * lax.rsqrt(jnp.mean(x * x, axis=1, keepdims=True) + epsilon))
    gains = []
    for b in range(0, width, 256):
        dn = mm_nt(mixed_ref[...], w_ref[b : b + 256, cols:])
        gain = jnp.zeros((1, 256), f32)
        for c in range(chunks):
            piece = dn[c * rows : (c + 1) * rows, :]
            out_refs[c][0:rows, b : b + 256] = piece.astype(bf16)
            gain = gain + jnp.sum(piece * units[c][:, b : b + 256], axis=0, keepdims=True)
        gains.append(gain)
    gain = jnp.concatenate(gains, axis=1)
    bias = pltpu.roll(bias, me * heads, 1)
    lanes = jnp.concatenate([sums[0], sums[1], bias, jnp.zeros((1, width - 2 * size - 128), f32)], axis=1)
    low = jnp.concatenate([gain, lanes, gm_ref[...], jnp.zeros((13, width), f32)], axis=0).astype(bf16)
    for c in range(chunks):
        out_refs[c][rows : rows + 16, :] = low


def middle_kernel(x_ref, gain_ref, *refs):
    middle = x_ref[...].astype(f32)
    for ref in refs[:-2]:
        middle = middle + ref[...].astype(f32)
    mid_ref, nm_ref = refs[-2:]
    mid_ref[...] = middle
    r = lax.rsqrt(jnp.mean(middle * middle, axis=1, keepdims=True) + epsilon)
    nm_ref[...] = (middle * r * gain_ref[...]).astype(bf16)


def norm_back(d, v, gain):
    r = lax.rsqrt(jnp.mean(v * v, axis=1, keepdims=True) + epsilon)
    u = v * r
    e = d * gain
    return r * (e - u * jnp.mean(e * u, axis=1, keepdims=True)), jnp.sum(d * u, axis=0, keepdims=True)


def middle_back_kernel(mid_ref, cot_ref, gain_ref, *refs):
    d = refs[0][...].astype(f32)
    for ref in refs[1:-3]:
        d = d + ref[...].astype(f32)
    dmid_ref, branch_ref, part_ref = refs[-3:]
    back, part = norm_back(d, mid_ref[...], gain_ref[...])
    back = back + cot_ref[...].astype(f32)
    dmid_ref[...] = back
    branch_ref[...] = back.astype(bf16)
    part_ref[...] = part


def weight_send_kernel(flip_ref, d_ref, out_ref):
    deep = out_ref.shape[2]
    other = 1 - lax.axis_index("ctx")
    for s in range(out_ref.shape[0]):
        out_ref[s] = mm(flip_ref[pl.ds(2 * s + other, 1)][0], d_ref[:, :deep]).astype(bf16)


def weight_keep_kernel(flip_ref, d_ref, got_ref, own_ref, *pair_refs):
    deep = got_ref.shape[2]
    me, half = lax.axis_index("shard"), lax.axis_index("ctx")
    for k in range(got_ref.shape[0]):
        total = mm(flip_ref[pl.ds(2 * (me ^ k) + half, 1)][0], d_ref[:, :deep])
        total = total + got_ref[pl.ds(me ^ k, 1)][0].astype(f32)
        if k == 0:
            own_ref[...] = total
        else:
            pair_refs[k - 1][...] = total.astype(bf16)


def finish_gates_kernel(in_ref, out_ref, gate_ref):
    cols = out_ref.shape[1]
    out_ref[...] = in_ref[:, :cols].astype(f32)
    gate_ref[...] = in_ref[:, cols:].astype(f32)


def finish_kernel(terms, x_ref, dmid_ref, gain_ref, ffn_ref, own_ref, *refs):
    dn_refs, refs = refs[:terms], refs[terms:]
    arrived, refs = refs[:-5], refs[-5:]
    in_ref, gu_ref, down_ref, qkv_ref, forget_ref = refs
    rows = x_ref.shape[0]
    d = dn_refs[0][0:rows, :].astype(f32)
    for ref in dn_refs[1:]:
        d = d + ref[0:rows, :].astype(f32)
    back, _ = norm_back(d, x_ref[...].astype(f32), gain_ref[...])
    in_ref[...] = (back + dmid_ref[...]).astype(bf16)
    units = down_ref.shape[1]
    gu_ref[:, 0, :] = ffn_ref[:, :units].astype(f32)
    gu_ref[:, 1, :] = ffn_ref[:, units : 2 * units].astype(f32)
    down_ref[...] = ffn_ref[:, 2 * units :].astype(f32)
    cols = qkv_ref.shape[2]
    total = own_ref[...]
    for ref in arrived:
        total = total + ref[...].astype(f32)
    for i in range(3):
        qkv_ref[i] = total[:, i * cols : (i + 1) * cols]
    forget_ref[...] = jnp.transpose(total[:, 3 * cols :])[: forget_ref.shape[0], :]


def body(tokens, cotangent, lengths, w_qkv, w_forget, forget_bias, w_ogate, w_out, w_gu, w_down, gain_attn, gain_mlp,
         qk_gain):
    slots, rows, width = tokens.shape
    assert slots == 1
    n = lax.axis_size("tp")
    me = lax.axis_index("tp")
    half = lax.axis_index("ctx")
    both = ("shard", "ctx")
    span = rows * n
    heads = w_forget.shape[1]
    size = qk_gain.shape[1]
    cols = heads * size
    units = w_down.shape[1]
    slab = w_qkv.shape[0]

    x_own = tokens[0]
    x_parts = gather_rows(x_own)

    own_pos = half * span + me * rows + jnp.arange(rows, dtype=jnp.int32)
    valid = (own_pos < lengths[0]).astype(f32)[:, None]
    cot_own = (cotangent[0].astype(f32) * valid).astype(bf16)
    cot = gather_all(after(cot_own, *x_parts))

    order = jnp.concatenate([(me ^ k) * rows + jnp.arange(rows, dtype=jnp.int32) for k in range(n)])
    rank, rank_t = order[:, None], order[None, :]

    first = jnp.concatenate(
        [w_out, w_qkv[:, 0], w_qkv[:, 1], w_qkv[:, 2], w_forget, jnp.zeros((slab, 128 - heads), bf16), w_ogate], axis=1
    )
    first = lax.all_gather(first, both, axis=0, tiled=True)
    rest = jnp.concatenate([w_gu.reshape(slab, 2 * units), w_down], axis=1)
    rest = lax.all_gather(rest, both, axis=0, tiled=True)
    wide = 4 * cols + 128
    w_out_full, out_block = first, (width, cols)
    if cols % 128:
        w_out_full = first[:, :cols]

    bias = lax.dynamic_slice_in_dim(forget_bias, me * heads, heads)
    bias = jnp.concatenate([bias, jnp.zeros((128 - heads,), f32)])[None, :]
    gain_a, gain_m = gain_attn[None, :], gain_mlp[None, :]
    qk_wide = jnp.tile(qk_gain, (1, heads))

    normed, qa, ka, va, sent, qraw, kraw, opener, pre, cum = call(
        functools.partial(project_kernel, heads, size, n),
        [
            sds((span, width), bf16),
            sds((span, heads * 128), bf16),
            sds((span, heads * 128), bf16),
            sds((span, heads * 128), bf16),
            sds((span, 2 * cols + 128), bf16),
            sds((span, cols), f32),
            sds((span, cols), f32),
            sds((span, cols), f32),
            sds((span, 128), f32),
            sds((span, 128), f32),
        ],
        *x_parts, first, gain_a, qk_wide, bias, rank, rank_t,
    )
    left = lax.ppermute(sent, "ctx", [(0, 1)])
    gated, attended, lse, kl, vl, *branch = call(
        functools.partial(attend_kernel, heads, size),
        [sds((span, cols), bf16), sds((span, cols), f32), sds((span, 128), f32)]
        + [sds((span, heads * 128), bf16)] * 2
        + [sds((rows, width), bf16)] * n,
        qa, ka, va, left, opener, rank, rank_t, w_out_full,
        blocks={7: out_block},
    )
    middle, nm_own = call(
        middle_kernel,
        [sds((rows, width), f32), sds((rows, width), bf16)],
        x_own, gain_m, *send_rows(after(branch, cot)),
    )
    tile = min(512, units)
    steps = units // tile
    d_hidden, cot, flip = call(
        functools.partial(hidden_back_kernel, n),
        [sds((span, units), f32), sds((span, width), bf16), sds((width, span), bf16)],
        after(cot, nm_own), normed, rest,
        grid=(steps,),
        in_specs=[whole((n, rows, width)), whole((span, width)), pl.BlockSpec((width, tile), lambda j: (0, j + 2 * steps))],
        out_specs=[pl.BlockSpec((span, tile), lambda j: (0, j)), whole((span, width)), whole((width, span))],
    )
    nm_parts = after(gather_rows(nm_own), d_hidden)
    nm, hidden, d_units, *p_parts = call(
        functools.partial(ffn_kernel, steps, n),
        [sds((span, width), bf16), sds((span, units), bf16), sds((span, 2 * units), bf16)]
        + [sds((rows, width), bf16)] * n,
        *nm_parts, d_hidden, rest, rest,
        grid=(steps,),
        in_specs=[whole((rows, width))] * n
        + [
            pl.BlockSpec((span, tile), lambda j: (0, j)),
            pl.BlockSpec((width, tile), lambda j: (0, j)),
            pl.BlockSpec((width, tile), lambda j: (0, j + steps)),
        ],
        out_specs=[whole((span, width)), pl.BlockSpec((span, tile), lambda j: (0, j)), whole((span, 2 * units))]
        + [whole((rows, width))] * n,
        scratch=[pltpu.VMEM((width, 2 * units), bf16)],
    )
    part_down = mm_tn(cot, hidden).astype(bf16)
    p_got = send_rows(p_parts, part_down)
    part_ffn = jnp.concatenate([mm_tn(nm, d_units).astype(bf16), part_down], axis=1)
    grad_ffn = lax.psum_scatter(after(part_ffn, p_got[1]), both, scatter_dimension=0, tiled=True)
    d_middle, db_own, gain_m_part = call(
        middle_back_kernel,
        [sds((rows, width), f32), sds((rows, width), bf16), sds((1, width), f32)],
        middle, cot_own, gain_m, *after(p_got, part_ffn),
    )
    db_parts = gather_rows(db_own)
    (down_rows,) = call(
        functools.partial(down_kernel, n),
        [sds((n, rows, width), bf16)],
        after(hidden, db_own), rest,
        blocks={1: (width, units)}, places={1: (0, 2)},
    )
    down = scatter_all(after(down_rows, db_parts))
    d_branch, dq, dk, dv, back, d_open, d_cum = call(
        functools.partial(attend_back_kernel, heads, size, n),
        [
            sds((span, width), bf16),
            sds((span, cols), f32),
            sds((span, cols), f32),
            sds((span, cols), f32),
            sds((span, 2 * cols + 128), bf16),
            sds((span, cols), bf16),
            sds((span, 128), f32),
        ],
        *after(db_parts, down_rows), qa, ka, va, kl, vl, cum, lse, opener, attended, rank, rank_t, w_out_full,
        blocks={n + 11: out_block}, weight=100,
    )
    part_gates = jnp.concatenate([mm_tn(d_branch, gated), mm_tn(normed, d_open)], axis=1).astype(bf16)
    back = lax.ppermute(back, "ctx", [(1, 0)])
    mixed, *dn = call(
        functools.partial(project_back_kernel, heads, size, n),
        [sds((span, wide), bf16)] + [sds((rows + 16, width), bf16)] * n,
        *x_parts, first, qk_wide, qraw, kraw, dq, dk, dv, back, d_open, d_cum, pre, rank, rank_t, gain_m_part,
    )
    down_sum = jnp.sum(after(down, mixed).astype(f32), axis=0)
    output = (valid * (middle + down_sum)).astype(bf16)
    deep = 3 * cols + 128
    grad_gates = lax.psum_scatter(after(part_gates, grad_ffn), both, scatter_dimension=0, tiled=True)
    shards = lax.axis_size("shard")
    flip = flip.reshape(2 * shards, slab, span)
    (sent,) = call(weight_send_kernel, [sds((shards, slab, deep), bf16)], flip, mixed)
    grad_own, *pairs = call(
        weight_keep_kernel,
        [sds((slab, deep), f32)] + [sds((slab, deep), bf16)] * (shards - 1),
        flip, mixed, swap(sent, "ctx", 1),
    )
    state_qkv = grad_own, [swap(p, "shard", k + 1) for k, p in enumerate(pairs)]
    dn = send_rows(after(dn, output))
    grad_out, grad_ogate = call(finish_gates_kernel, [sds((slab, cols), f32)] * 2, grad_gates, weight=100)
    input_grad, grad_gu, grad_down, grad_qkv, grad_forget = call(
        functools.partial(finish_kernel, len(dn)),
        [
            sds((rows, width), bf16),
            sds((slab, 2, units), f32),
            sds((slab, units), f32),
            sds((3, slab, cols), f32),
            sds((heads, slab), f32),
        ],
        x_own, d_middle, gain_a, grad_ffn, state_qkv[0], *dn, *state_qkv[1],
    )
    grad_qkv, grad_forget = jnp.swapaxes(grad_qkv, 0, 1), jnp.swapaxes(grad_forget, 0, 1)

    sums = sum(g[rows:].astype(f32) for g in dn)
    small = jnp.concatenate([sums[0], sums[1, : 2 * size + n * heads], sums[2]])
    small = sum_over(small, ("ctx", "shard"))
    edges = [0, width, width + 2 * size, width + 2 * size + n * heads]
    return (
        output[None],
        input_grad[None],
        grad_qkv,
        grad_forget,
        small[edges[2] : edges[3]],
        grad_ogate,
        grad_out,
        grad_gu,
        grad_down,
        small[edges[0] : edges[1]],
        small[edges[2] + n * heads :],
        small[edges[1] : edges[2]].reshape(2, size),
    )


def solution(mesh):
    rows = P("shard", ("ctx", "tp"), None)
    flat = P(("shard", "ctx"), "tp")
    deep = P(("shard", "ctx"), None, "tp")
    return jax.shard_map(
        body,
        mesh=mesh,
        in_specs=(rows, rows, P("shard"), deep, flat, P(), flat, flat, deep, flat, P(), P(), P()),
        out_specs=(rows, rows, deep, flat, P(), flat, flat, deep, flat, P(), P(), P()),
        check_vma=False,
    )
```

```python
import functools
import math

import jax
import jax.numpy as jnp
from jax import lax
from jax.experimental import pallas as pl
from jax.experimental.pallas import tpu as pltpu
from jax.sharding import PartitionSpec as P

epsilon = 1e-06
f32 = jnp.float32
bf16 = jnp.bfloat16
BIG = 1e30
VMEM_LIMIT = 60 * 1024 * 1024


def mm(left, right):
    return jnp.dot(left, right, preferred_element_type=f32)


def mm_nt(left, right):
    return lax.dot_general(left, right, (((1,), (1,)), ((), ())), preferred_element_type=f32)


def mm_tn(left, right):
    return lax.dot_general(left, right, (((0,), (0,)), ((), ())), preferred_element_type=f32)


def whole(shape):
    return pl.BlockSpec(shape, lambda *_: (0,) * len(shape))


def call(kernel, outs, *operands, grid=None, in_specs=None, out_specs=None, scratch=(), blocks=None, places=None,
         weight=0.1):
    extra = {}
    if grid is None and blocks:
        grid = (1,)
        places = places or {}
        in_specs = [
            pl.BlockSpec(blocks.get(i, o.shape), functools.partial(lambda at, *_: at, places.get(i, (0,) * o.ndim)))
            for i, o in enumerate(operands)
        ]
        out_specs = [whole(o.shape) for o in outs]
    if grid is not None:
        extra = dict(grid=grid, in_specs=in_specs, out_specs=out_specs)
    return pl.pallas_call(
        kernel,
        out_shape=outs,
        scratch_shapes=list(scratch),
        compiler_params=pltpu.CompilerParams(vmem_limit_bytes=VMEM_LIMIT),
        cost_estimate=pl.CostEstimate(flops=int(weight * 1e9), bytes_accessed=int(weight * 1e6), transcendentals=0),
        **extra,
    )(*operands)


def sds(shape, dtype):
    return jax.ShapeDtypeStruct(shape, dtype)


def swap(value, axis, bit):
    n = lax.axis_size(axis)
    return lax.ppermute(value, axis, [(j, j ^ bit) for j in range(n)])


def gather_rows(own):
    n = lax.axis_size("tp")
    if n != 4:
        return [own] + [swap(own, "tp", k) for k in range(1, n)]
    far = swap(own, "tp", 2)
    near = swap(own, "tp", 1)
    return [own, near, far, swap(far, "tp", 1)]


def gather_all(own):
    n = lax.axis_size("tp")
    return lax.all_to_all(jnp.broadcast_to(own[None], (n,) + own.shape), "tp", 0, 0, tiled=True)


def scatter_all(blocks):
    return lax.all_to_all(blocks, "tp", 0, 0, tiled=True)


def send_rows(parts, *late):
    n = lax.axis_size("tp")
    if n != 4:
        return [parts[0]] + [swap(parts[k], "tp", k) for k in range(1, n)]
    across = swap(parts[3], "tp", 1)
    near = swap(after(parts[1], *late) if late else parts[1], "tp", 1)
    far = (parts[2].astype(f32) + across.astype(f32)).astype(bf16)
    return [parts[0], near, swap(far, "tp", 2)]


def after(value, *others):
    return lax.optimization_barrier((value, others))[0]


def sum_over(value, axes):
    for axis in axes:
        n = lax.axis_size(axis)
        total = value
        for k in range(1, n):
            total = total + swap(value, axis, k)
        value = total
    return value


def thirds(value):
    high = value.astype(bf16)
    rest = value - high.astype(f32)
    middle = rest.astype(bf16)
    return high, middle, (rest - middle.astype(f32)).astype(bf16)


def head_sums(value, size):
    cols = value.shape[1]
    shape = (cols, cols)
    row = lax.broadcasted_iota(jnp.int32, shape, 0) // size
    col = lax.broadcasted_iota(jnp.int32, shape, 1) // size
    same = (row == col).astype(bf16)
    high = value.astype(bf16)
    low = (value - high.astype(f32)).astype(bf16)
    return mm(high, same) + mm(low, same)


def spread(pieces, rows):
    used = sum(p.shape[1] for p in pieces)
    return jnp.concatenate(list(pieces) + [jnp.zeros((rows, 128 - used), bf16)], axis=1)


def running(mask, value, heads):
    rows = value.shape[0]
    parts = thirds(value[:, :heads])
    total = mm(mask, spread(parts, rows))
    return total[:, :heads] + total[:, heads : 2 * heads] + total[:, 2 * heads : 3 * heads]


def norm_kernel(gain_ref, *refs):
    normed_ref = refs[-1]
    rows = refs[0].shape[0]
    for c, x_ref in enumerate(refs[:-1]):
        x = x_ref[...].astype(f32)
        r = lax.rsqrt(jnp.mean(x * x, axis=1, keepdims=True) + epsilon)
        normed_ref[c * rows : (c + 1) * rows, :] = (x * r * gain_ref[...]).astype(bf16)


def project_kernel(heads, size, *refs):
    normed_ref, w_ref, qk_ref, bias_ref, rank_ref, rank_t_ref = refs[:6]
    (qa_ref, ka_ref, va_ref, send_ref, qraw_ref, kraw_ref, open_ref, pre_ref, cum_ref) = refs[6:]
    span = normed_ref.shape[0]
    cols = heads * size
    normed = normed_ref[...]
    pre = mm(normed, w_ref[:, 4 * cols : 4 * cols + 128]) + bias_ref[...]
    pre_ref[...] = pre
    logs = jnp.minimum(pre, 0.0) - jnp.log(1.0 + jnp.exp(-jnp.abs(pre)))
    earlier = (rank_t_ref[...] <= rank_ref[...]).astype(bf16)
    cum = running(earlier, logs, heads)
    cum_ref[...] = jnp.concatenate([cum, jnp.zeros((span, 128 - heads), f32)], axis=1)
    ones = jnp.ones((span, 3), bf16)
    fill = jnp.zeros((span, 128 - size - 6), bf16)
    cums = thirds(cum)
    outs = thirds(-cum)
    fars = thirds(jnp.sum(logs[:, :heads], axis=0, keepdims=True) - cum)

    def at(parts, h):
        return [p[:, h : h + 1] for p in parts]

    for which, raw_ref in ((0, qraw_ref), (1, kraw_ref)):
        raw = mm(normed, w_ref[:, (which + 1) * cols : (which + 2) * cols])
        raw_ref[...] = raw
        r = lax.rsqrt(head_sums(raw * raw, size) * (1.0 / size) + epsilon)
        value = (raw * r * qk_ref[which : which + 1, :]).astype(bf16)
        if which == 0:
            value = value * jnp.asarray(1.0 / math.sqrt(size), bf16)
            for h in range(heads):
                piece = value[:, h * size : (h + 1) * size]
                qa_ref[:, h * 128 : (h + 1) * 128] = jnp.concatenate([piece] + at(cums, h) + [ones, fill], axis=1)
        else:
            send_ref[:, 0:cols] = value
            for h in range(heads):
                piece = value[:, h * size : (h + 1) * size]
                ka_ref[:, h * 128 : (h + 1) * 128] = jnp.concatenate([piece, ones] + at(outs, h) + [fill], axis=1)
    value = mm(normed, w_ref[:, 3 * cols : 4 * cols]).astype(bf16)
    send_ref[:, cols : 2 * cols] = value
    tail = jnp.concatenate([ones, jnp.zeros((span, 128 - size - 3), bf16)], axis=1)
    for h in range(heads):
        va_ref[:, h * 128 : (h + 1) * 128] = jnp.concatenate([value[:, h * size : (h + 1) * size], tail], axis=1)
    send_ref[:, 2 * cols :] = spread(fars, span)
    open_ref[...] = jax.nn.sigmoid(mm(normed, w_ref[:, 4 * cols + 128 :]))


def attend_kernel(heads, size, qa_ref, ka_ref, va_ref, left_ref, open_ref, rank_ref, rank_t_ref, wout_ref,
                  gated_ref, att_ref, lse_ref, kl_ref, vl_ref, *branch_refs):
    cols = heads * size
    rows = qa_ref.shape[0]
    chunks = len(branch_refs)
    step = rows // chunks
    keep = rank_t_ref[...] <= rank_ref[...]
    shut = jnp.where(lax.axis_index("ctx") == 0, -BIG, 0.0).astype(bf16)
    ones = jnp.ones((rows, 3), bf16)
    fill = jnp.zeros((rows, 128 - size - 6), bf16)
    tail = jnp.zeros((rows, 128 - size - 3), bf16)
    lses = []
    for h in range(heads):
        wide = slice(h * 128, (h + 1) * 128)
        hs = slice(h * size, (h + 1) * size)
        far = [left_ref[:, 2 * cols + i * heads + h : 2 * cols + i * heads + h + 1] for i in range(3)]
        kl = jnp.concatenate([left_ref[:, hs], ones, far[0] + shut, far[1], far[2], fill], axis=1)
        vl = jnp.concatenate([left_ref[:, cols + h * size : cols + (h + 1) * size], ones, tail], axis=1)
        kl_ref[:, wide] = kl
        vl_ref[:, wide] = vl
        q = qa_ref[:, wide]
        el = jnp.exp(mm_nt(q, kl)).astype(bf16)
        er = jnp.exp(jnp.where(keep, mm_nt(q, ka_ref[:, wide]), -BIG)).astype(bf16)
        o = mm(el, vl) + mm(er, va_ref[:, wide])
        total = o[:, size : size + 1]
        att = o[:, :size] / total
        att_ref[:, hs] = att
        gated_ref[:, hs] = (att * open_ref[:, hs]).astype(bf16)
        lses.append(jnp.log(total))
    lse_ref[...] = jnp.concatenate(lses + [jnp.zeros((rows, 128 - heads), f32)], axis=1)
    branch = mm_nt(gated_ref[...], wout_ref[...]).astype(bf16)
    for c in range(chunks):
        branch_refs[c][...] = branch[c * step : (c + 1) * step, :]


def hidden_back_kernel(chunks, cot_ref, normed_ref, wd_ref, dh_ref, order_ref, flip_ref):
    me = lax.axis_index("tp")
    rows = cot_ref.shape[1]

    @pl.when(pl.program_id(0) == 0)
    def _():
        for c in range(chunks):
            order_ref[c * rows : (c + 1) * rows, :] = cot_ref[pl.ds(me ^ c, 1)][0]
        flip_ref[...] = jnp.transpose(normed_ref[...])

    dh_ref[...] = mm(order_ref[...], wd_ref[...])


def ffn_kernel(steps, chunks, *refs):
    nm_refs, refs = refs[:chunks], refs[chunks:]
    dh_ref, wg_ref, wu_ref, nm_ref, hid_ref, dgu_ref = refs[:6]
    p_refs, refs = refs[6 : 6 + chunks], refs[6 + chunks :]
    w_all = refs[0]
    rows = nm_refs[0].shape[0]
    tile = wg_ref.shape[1]
    units = tile * steps
    j = pl.program_id(0)

    @pl.when(j == 0)
    def _():
        for c in range(chunks):
            nm_ref[c * rows : (c + 1) * rows, :] = nm_refs[c][...]

    gate = mm(nm_ref[...], wg_ref[...])
    up = mm(nm_ref[...], wu_ref[...])
    dh = dh_ref[...]
    sig = jax.nn.sigmoid(gate)
    act = gate * sig
    hid_ref[...] = (act * up).astype(bf16)
    dg = (dh * up * sig * (1.0 + gate * (1.0 - sig))).astype(bf16)
    du = (dh * act).astype(bf16)
    for s in range(steps):

        @pl.when(j == s)
        def _():
            at, up_at = slice(s * tile, (s + 1) * tile), slice(units + s * tile, units + (s + 1) * tile)
            dgu_ref[:, at] = dg
            dgu_ref[:, up_at] = du
            w_all[:, at] = wg_ref[...]
            w_all[:, up_at] = wu_ref[...]

    @pl.when(j == steps - 1)
    def _():
        width = w_all.shape[0]
        for b in range(0, width, 256):
            part = mm_nt(dgu_ref[...], w_all[b : b + 256, :]).astype(bf16)
            for c in range(chunks):
                p_refs[c][:, b : b + 256] = part[c * rows : (c + 1) * rows, :]


def down_kernel(chunks, hid_ref, wd_ref, out_ref):
    me = lax.axis_index("tp")
    down = mm_nt(hid_ref[...], wd_ref[...]).astype(bf16)
    rows = out_ref.shape[1]
    for c in range(chunks):
        out_ref[pl.ds(me ^ c, 1)] = down[c * rows : (c + 1) * rows, :][None]


def attend_back_kernel(heads, size, chunks, *refs):
    db_refs, refs = refs[:chunks], refs[chunks:]
    (qa_ref, ka_ref, va_ref, kl_ref, vl_ref, cum_ref, lse_ref, open_ref, att_ref, rank_ref, rank_t_ref,
     wout_ref) = refs[:12]
    branch_ref, dq_ref, dk_ref, dv_ref, back_ref, dopen_ref, dcum_ref = refs[12:]
    cols = heads * size
    part = db_refs[0].shape[0]
    rows = part * chunks
    for c in range(chunks):
        branch_ref[c * part : (c + 1) * part, :] = db_refs[c][...]
    keep = rank_t_ref[...] >= rank_ref[...]
    dg = mm(branch_ref[...], wout_ref[...])
    op = open_ref[...]
    att = att_ref[...]
    dopen_ref[...] = (dg * att * op * (1.0 - op)).astype(bf16)
    da_all = (dg * op).astype(bf16)
    prod = da_all.astype(f32) * att
    place = thirds(cum_ref[:, :heads] - lse_ref[:, :heads])
    ones = jnp.ones((rows, 3), bf16)
    fill = jnp.zeros((rows, 128 - size - 6), bf16)
    tail = jnp.zeros((rows, 128 - size - 3), bf16)
    owns, lefts = [], []
    for h in range(heads):
        wide = slice(h * 128, (h + 1) * 128)
        hs = slice(h * size, (h + 1) * size)
        vs = slice(cols + h * size, cols + (h + 1) * size)
        q = jnp.concatenate([qa_ref[:, h * 128 : h * 128 + size]] + [p[:, h : h + 1] for p in place] + [ones, fill], axis=1)
        delta = thirds(-jnp.sum(prod[:, hs], axis=1, keepdims=True))
        da = jnp.concatenate([da_all[:, hs], delta[0], delta[1], delta[2], tail], axis=1)
        dq = jnp.zeros((rows, 128), f32)
        found = []
        for k_ref, v_ref, right in ((kl_ref, vl_ref, False), (ka_ref, va_ref, True)):
            k, v = k_ref[:, wide], v_ref[:, wide]
            score = mm_nt(k, q)
            if right:
                score = jnp.where(keep, score, -BIG)
            p = jnp.exp(score)
            ds = (p * mm_nt(v, da)).astype(bf16)
            found += [mm(p.astype(bf16), da)[:, :size], mm(ds, q)]
            dq = dq + mm_tn(ds, k)
        dq_ref[:, hs] = dq[:, :size] * (1.0 / math.sqrt(size))
        back_ref[:, vs] = found[0].astype(bf16)
        back_ref[:, hs] = found[1][:, :size].astype(bf16)
        dv_ref[:, hs] = found[2]
        dk_ref[:, hs] = found[3][:, :size]
        lefts.append(-found[1][:, size + 3 : size + 4])
        owns.append(dq[:, size : size + 1] - found[3][:, size + 3 : size + 4])
    own = jnp.concatenate(owns, axis=1)
    dcum_ref[...] = jnp.concatenate([own, jnp.zeros((rows, 128 - heads), f32)], axis=1)
    total = jnp.broadcast_to(jnp.sum(own, axis=0, keepdims=True), (rows, heads))
    sent = thirds(jnp.concatenate(lefts, axis=1)) + thirds(total)
    back_ref[:, 2 * cols :] = spread(sent, rows)


def project_back_kernel(heads, size, *refs):
    (normed_ref, gain_ref, w_ref, qk_ref, qraw_ref, kraw_ref, dq_ref, dk_ref, dv_ref, back_ref, dopen_ref, dcum_ref, pre_ref, rank_ref,
     rank_t_ref, gm_ref) = refs[:16]
    mixed_ref, out_refs = refs[16], refs[17:]
    cols = heads * size
    span, width = normed_ref.shape
    chunks = len(out_refs)
    rows = span // chunks
    sums = []
    for which, raw_ref in ((0, qraw_ref), (1, kraw_ref)):
        d = dq_ref[...] if which == 0 else dk_ref[...] + back_ref[:, :cols].astype(f32)
        raw = raw_ref[...]
        r = lax.rsqrt(head_sums(raw * raw, size) * (1.0 / size) + epsilon)
        u = raw * r
        total = jnp.sum(d * u, axis=0, keepdims=True)
        sums.append(sum(total[:, h * size : (h + 1) * size] for h in range(heads)))
        e = d * qk_ref[which : which + 1, :]
        mixed_ref[:, which * cols : (which + 1) * cols] = (
            r * (e - u * (head_sums(e * u, size) * (1.0 / size)))
        ).astype(bf16)
    mixed_ref[:, 2 * cols : 3 * cols] = (dv_ref[...] + back_ref[:, cols : 2 * cols].astype(f32)).astype(bf16)
    mixed_ref[:, 3 * cols + 128 :] = dopen_ref[...]
    extra = back_ref[:, 2 * cols :].astype(f32)
    got = extra[:, :heads] + extra[:, heads : 2 * heads] + extra[:, 2 * heads : 3 * heads]
    after_sum = extra[:, 3 * heads : 4 * heads] + extra[:, 4 * heads : 5 * heads] + extra[:, 5 * heads : 6 * heads]
    later = (rank_t_ref[...] >= rank_ref[...]).astype(bf16)
    dlog = running(later, dcum_ref[:, :heads] + got, heads) + after_sum
    df = jnp.concatenate([dlog, jnp.zeros((span, 128 - heads), f32)], axis=1) * jax.nn.sigmoid(-pre_ref[...])
    bias = jnp.sum(df, axis=0, keepdims=True)
    mixed_ref[:, 3 * cols : 3 * cols + 128] = df.astype(bf16)
    me = lax.axis_index("tp")
    gains = []
    for b in range(0, width, 256):
        dn = mm_nt(mixed_ref[...], w_ref[b : b + 256, cols:])
        for c in range(chunks):
            out_refs[c][0:rows, b : b + 256] = dn[c * rows : (c + 1) * rows, :].astype(bf16)
        gain = jnp.sum(dn * normed_ref[:, b : b + 256].astype(f32), axis=0, keepdims=True)
        gains.append(gain)
    gain = jnp.concatenate(gains, axis=1) / gain_ref[...]
    bias = pltpu.roll(bias, me * heads, 1)
    lanes = jnp.concatenate([sums[0], sums[1], bias, jnp.zeros((1, width - 2 * size - 128), f32)], axis=1)
    low = jnp.concatenate([gain, lanes, gm_ref[...], jnp.zeros((13, width), f32)], axis=0).astype(bf16)
    for c in range(chunks):
        out_refs[c][rows : rows + 16, :] = low


def middle_kernel(x_ref, gain_ref, *refs):
    middle = x_ref[...].astype(f32)
    for ref in refs[:-2]:
        middle = middle + ref[...].astype(f32)
    mid_ref, nm_ref = refs[-2:]
    mid_ref[...] = middle
    r = lax.rsqrt(jnp.mean(middle * middle, axis=1, keepdims=True) + epsilon)
    nm_ref[...] = (middle * r * gain_ref[...]).astype(bf16)


def norm_back(d, v, gain):
    r = lax.rsqrt(jnp.mean(v * v, axis=1, keepdims=True) + epsilon)
    u = v * r
    e = d * gain
    return r * (e - u * jnp.mean(e * u, axis=1, keepdims=True)), jnp.sum(d * u, axis=0, keepdims=True)


def middle_back_kernel(mid_ref, cot_ref, gain_ref, *refs):
    d = refs[0][...].astype(f32)
    for ref in refs[1:-3]:
        d = d + ref[...].astype(f32)
    dmid_ref, branch_ref, part_ref = refs[-3:]
    back, part = norm_back(d, mid_ref[...], gain_ref[...])
    back = back + cot_ref[...].astype(f32)
    dmid_ref[...] = back
    branch_ref[...] = back.astype(bf16)
    part_ref[...] = part


def weight_send_kernel(flip_ref, d_ref, out_ref):
    deep = out_ref.shape[2]
    other = 1 - lax.axis_index("ctx")
    for s in range(out_ref.shape[0]):
        out_ref[s] = mm(flip_ref[pl.ds(2 * s + other, 1)][0], d_ref[:, :deep]).astype(bf16)


def weight_keep_kernel(flip_ref, d_ref, got_ref, own_ref, *pair_refs):
    deep = got_ref.shape[2]
    me, half = lax.axis_index("shard"), lax.axis_index("ctx")
    for k in range(got_ref.shape[0]):
        total = mm(flip_ref[pl.ds(2 * (me ^ k) + half, 1)][0], d_ref[:, :deep])
        total = total + got_ref[pl.ds(me ^ k, 1)][0].astype(f32)
        if k == 0:
            own_ref[...] = total
        else:
            pair_refs[k - 1][...] = total.astype(bf16)


def finish_gates_kernel(in_ref, out_ref, gate_ref):
    cols = out_ref.shape[1]
    out_ref[...] = in_ref[:, :cols].astype(f32)
    gate_ref[...] = in_ref[:, cols:].astype(f32)


def finish_kernel(terms, x_ref, dmid_ref, gain_ref, ffn_ref, own_ref, *refs):
    dn_refs, refs = refs[:terms], refs[terms:]
    arrived, refs = refs[:-5], refs[-5:]
    in_ref, gu_ref, down_ref, qkv_ref, forget_ref = refs
    rows = x_ref.shape[0]
    d = dn_refs[0][0:rows, :].astype(f32)
    for ref in dn_refs[1:]:
        d = d + ref[0:rows, :].astype(f32)
    back, _ = norm_back(d, x_ref[...].astype(f32), gain_ref[...])
    in_ref[...] = (back + dmid_ref[...]).astype(bf16)
    units = down_ref.shape[1]
    gu_ref[:, 0, :] = ffn_ref[:, :units].astype(f32)
    gu_ref[:, 1, :] = ffn_ref[:, units : 2 * units].astype(f32)
    down_ref[...] = ffn_ref[:, 2 * units :].astype(f32)
    cols = qkv_ref.shape[2]
    total = own_ref[...]
    for ref in arrived:
        total = total + ref[...].astype(f32)
    for i in range(3):
        qkv_ref[i] = total[:, i * cols : (i + 1) * cols]
    forget_ref[...] = jnp.transpose(total[:, 3 * cols :])[: forget_ref.shape[0], :]


def body(tokens, cotangent, lengths, w_qkv, w_forget, forget_bias, w_ogate, w_out, w_gu, w_down, gain_attn, gain_mlp,
         qk_gain):
    slots, rows, width = tokens.shape
    assert slots == 1
    n = lax.axis_size("tp")
    me = lax.axis_index("tp")
    half = lax.axis_index("ctx")
    both = ("shard", "ctx")
    span = rows * n
    heads = w_forget.shape[1]
    size = qk_gain.shape[1]
    cols = heads * size
    units = w_down.shape[1]
    slab = w_qkv.shape[0]

    x_own = tokens[0]
    x_parts = gather_rows(x_own)

    own_pos = half * span + me * rows + jnp.arange(rows, dtype=jnp.int32)
    valid = (own_pos < lengths[0]).astype(f32)[:, None]
    cot_own = (cotangent[0].astype(f32) * valid).astype(bf16)
    cot = gather_all(after(cot_own, *x_parts))

    order = jnp.concatenate([(me ^ k) * rows + jnp.arange(rows, dtype=jnp.int32) for k in range(n)])
    rank, rank_t = order[:, None], order[None, :]

    first = jnp.concatenate(
        [w_out, w_qkv[:, 0], w_qkv[:, 1], w_qkv[:, 2], w_forget, jnp.zeros((slab, 128 - heads), bf16), w_ogate], axis=1
    )
    first = lax.all_gather(first, both, axis=0, tiled=True)
    rest = jnp.concatenate([w_gu.reshape(slab, 2 * units), w_down], axis=1)
    rest = lax.all_gather(rest, both, axis=0, tiled=True)
    wide = 4 * cols + 128
    w_out_full, out_block = first, (width, cols)
    if cols % 128:
        w_out_full = first[:, :cols]

    bias = lax.dynamic_slice_in_dim(forget_bias, me * heads, heads)
    bias = jnp.concatenate([bias, jnp.zeros((128 - heads,), f32)])[None, :]
    gain_a, gain_m = gain_attn[None, :], gain_mlp[None, :]
    qk_wide = jnp.tile(qk_gain, (1, heads))

    (normed,) = call(norm_kernel, [sds((span, width), bf16)], gain_a, *x_parts)
    qa, ka, va, sent, qraw, kraw, opener, pre, cum = call(
        functools.partial(project_kernel, heads, size),
        [
            sds((span, heads * 128), bf16),
            sds((span, heads * 128), bf16),
            sds((span, heads * 128), bf16),
            sds((span, 2 * cols + 128), bf16),
            sds((span, cols), f32),
            sds((span, cols), f32),
            sds((span, cols), f32),
            sds((span, 128), f32),
            sds((span, 128), f32),
        ],
        normed, first, qk_wide, bias, rank, rank_t,
    )
    left = lax.ppermute(sent, "ctx", [(0, 1)])
    gated, attended, lse, kl, vl, *branch = call(
        functools.partial(attend_kernel, heads, size),
        [sds((span, cols), bf16), sds((span, cols), f32), sds((span, 128), f32)]
        + [sds((span, heads * 128), bf16)] * 2
        + [sds((rows, width), bf16)] * n,
        qa, ka, va, left, opener, rank, rank_t, w_out_full,
        blocks={7: out_block},
    )
    middle, nm_own = call(
        middle_kernel,
        [sds((rows, width), f32), sds((rows, width), bf16)],
        x_own, gain_m, *send_rows(after(branch, cot)),
    )
    tile = min(512, units)
    steps = units // tile
    d_hidden, cot, flip = call(
        functools.partial(hidden_back_kernel, n),
        [sds((span, units), f32), sds((span, width), bf16), sds((width, span), bf16)],
        after(cot, nm_own), normed, rest,
        grid=(steps,),
        in_specs=[whole((n, rows, width)), whole((span, width)), pl.BlockSpec((width, tile), lambda j: (0, j + 2 * steps))],
        out_specs=[pl.BlockSpec((span, tile), lambda j: (0, j)), whole((span, width)), whole((width, span))],
    )
    nm_parts = after(gather_rows(nm_own), d_hidden)
    nm, hidden, d_units, *p_parts = call(
        functools.partial(ffn_kernel, steps, n),
        [sds((span, width), bf16), sds((span, units), bf16), sds((span, 2 * units), bf16)]
        + [sds((rows, width), bf16)] * n,
        *nm_parts, d_hidden, rest, rest,
        grid=(steps,),
        in_specs=[whole((rows, width))] * n
        + [
            pl.BlockSpec((span, tile), lambda j: (0, j)),
            pl.BlockSpec((width, tile), lambda j: (0, j)),
            pl.BlockSpec((width, tile), lambda j: (0, j + steps)),
        ],
        out_specs=[whole((span, width)), pl.BlockSpec((span, tile), lambda j: (0, j)), whole((span, 2 * units))]
        + [whole((rows, width))] * n,
        scratch=[pltpu.VMEM((width, 2 * units), bf16)],
    )
    part_down = mm_tn(cot, hidden).astype(bf16)
    p_got = send_rows(p_parts, part_down)
    part_ffn = jnp.concatenate([mm_tn(nm, d_units).astype(bf16), part_down], axis=1)
    grad_ffn = lax.psum_scatter(after(part_ffn, p_got[1]), both, scatter_dimension=0, tiled=True)
    d_middle, db_own, gain_m_part = call(
        middle_back_kernel,
        [sds((rows, width), f32), sds((rows, width), bf16), sds((1, width), f32)],
        middle, cot_own, gain_m, *after(p_got, part_ffn),
    )
    db_parts = gather_rows(db_own)
    (down_rows,) = call(
        functools.partial(down_kernel, n),
        [sds((n, rows, width), bf16)],
        after(hidden, db_own), rest,
        blocks={1: (width, units)}, places={1: (0, 2)},
    )
    down = scatter_all(after(down_rows, db_parts))
    d_branch, dq, dk, dv, back, d_open, d_cum = call(
        functools.partial(attend_back_kernel, heads, size, n),
        [
            sds((span, width), bf16),
            sds((span, cols), f32),
            sds((span, cols), f32),
            sds((span, cols), f32),
            sds((span, 2 * cols + 128), bf16),
            sds((span, cols), bf16),
            sds((span, 128), f32),
        ],
        *after(db_parts, down_rows), qa, ka, va, kl, vl, cum, lse, opener, attended, rank, rank_t, w_out_full,
        blocks={n + 11: out_block}, weight=100,
    )
    part_gates = jnp.concatenate([mm_tn(d_branch, gated), mm_tn(normed, d_open)], axis=1).astype(bf16)
    back = lax.ppermute(back, "ctx", [(1, 0)])
    mixed, *dn = call(
        functools.partial(project_back_kernel, heads, size),
        [sds((span, wide), bf16)] + [sds((rows + 16, width), bf16)] * n,
        normed, gain_a, first, qk_wide, qraw, kraw, dq, dk, dv, back, d_open, d_cum, pre, rank, rank_t, gain_m_part,
    )
    down_sum = jnp.sum(after(down, mixed).astype(f32), axis=0)
    output = (valid * (middle + down_sum)).astype(bf16)
    deep = 3 * cols + 128
    grad_gates = lax.psum_scatter(after(part_gates, grad_ffn), both, scatter_dimension=0, tiled=True)
    shards = lax.axis_size("shard")
    flip = flip.reshape(2 * shards, slab, span)
    (sent,) = call(weight_send_kernel, [sds((shards, slab, deep), bf16)], flip, mixed)
    grad_own, *pairs = call(
        weight_keep_kernel,
        [sds((slab, deep), f32)] + [sds((slab, deep), bf16)] * (shards - 1),
        flip, mixed, swap(sent, "ctx", 1),
    )
    state_qkv = grad_own, [swap(p, "shard", k + 1) for k, p in enumerate(pairs)]
    dn = send_rows(after(dn, output))
    grad_out, grad_ogate = call(finish_gates_kernel, [sds((slab, cols), f32)] * 2, grad_gates, weight=100)
    input_grad, grad_gu, grad_down, grad_qkv, grad_forget = call(
        functools.partial(finish_kernel, len(dn)),
        [
            sds((rows, width), bf16),
            sds((slab, 2, units), f32),
            sds((slab, units), f32),
            sds((3, slab, cols), f32),
            sds((heads, slab), f32),
        ],
        x_own, d_middle, gain_a, grad_ffn, state_qkv[0], *dn, *state_qkv[1],
    )
    grad_qkv, grad_forget = jnp.swapaxes(grad_qkv, 0, 1), jnp.swapaxes(grad_forget, 0, 1)

    sums = sum(g[rows:].astype(f32) for g in dn)
    small = jnp.concatenate([sums[0], sums[1, : 2 * size + n * heads], sums[2]])
    small = sum_over(small, ("ctx", "shard"))
    edges = [0, width, width + 2 * size, width + 2 * size + n * heads]
    return (
        output[None],
        input_grad[None],
        grad_qkv,
        grad_forget,
        small[edges[2] : edges[3]],
        grad_ogate,
        grad_out,
        grad_gu,
        grad_down,
        small[edges[0] : edges[1]],
        small[edges[2] + n * heads :],
        small[edges[1] : edges[2]].reshape(2, size),
    )


def solution(mesh):
    rows = P("shard", ("ctx", "tp"), None)
    flat = P(("shard", "ctx"), "tp")
    deep = P(("shard", "ctx"), None, "tp")
    return jax.shard_map(
        body,
        mesh=mesh,
        in_specs=(rows, rows, P("shard"), deep, flat, P(), flat, flat, deep, flat, P(), P(), P()),
        out_specs=(rows, rows, deep, flat, P(), flat, flat, deep, flat, P(), P(), P()),
        check_vma=False,
    )
```
